32 devices in a mesh: groups: 2 (over x), seq: 8 (over z, y), head: 2 (over core).
Axes of the slice: x: 2, y: 2, z: 4, core: 2. Of those that a mesh axis runs over, the one named last changes fastest.
Arguments:
- queries: bfloat16 [8192, 2048], P(('groups', 'seq'), 'head'), parts along dimension 0, may hold values from -6 to 6
- keys: bfloat16 [8192, 1024], P(('groups', 'seq'), 'head'), parts along dimension 0, may hold values from -6 to 6
- values: bfloat16 [8192, 1024], P(('groups', 'seq'), 'head'), parts along dimension 0, may hold values from -6 to 6
- segments: int32 [8192], P('groups'), parts along dimension 0, may hold values from 0 to 7, never falling along the last dimension, each value on 1 to 1024 neighbouring positions
- out_weight: bfloat16 [2048, 5376], P('head'), may hold values from -0.125 to 0.125
Outputs:
- mixed: bfloat16 [8192, 5376], P(('groups', 'seq')), parts along dimension 0
The draws below stay inside these ranges and needn't reach their ends.
There are 2 independent parts, one for each index of `groups`. The reference program is written for one: setup_inputs(seed, part) draws one part's arguments, and reference() takes and returns one part's arrays. A program takes and returns all parts, laid end to end along the dimension named above; an argument that names none is the same for every part. Nothing has to cross between parts.
Inputs may be any that keep to these rules, and one draw needn't show every extreme that they name: `segments`: document ids never fall along the slab; each document has 1 to 1024 tokens, one exactly 1024.
All inputs are finite; a program needn't handle non-finite values.
Results may differ from the reference program's by a relative error of at most 0.011.
Values may be sent and summed in bfloat16 or wider, within the bound.
A program may use at most 128 MiB of HBM per device.

```python
import math
import jax
import jax.numpy as jnp
import numpy as np
from jax import lax

D = 5376
QUERY_HEADS = 16
KEY_VALUE_HEADS = 8
HEAD_SIZE = 128
SCALAR = 168
ATTENTION_SPAN = 1024
SLAB_TOKENS = 4096


def draw_keys(key, part):
    final_output = jnp.clip(jax.random.normal(jax.random.fold_in(key, 11), (SLAB_TOKENS, KEY_VALUE_HEADS * HEAD_SIZE), jnp.float32), -6.0, 6.0)
    return final_output.astype(jnp.bfloat16)


def draw_queries(key, part):
    final_output = jnp.clip(jax.random.normal(jax.random.fold_in(key, 21), (SLAB_TOKENS, QUERY_HEADS * HEAD_SIZE), jnp.float32), -6.0, 6.0)
    return final_output.astype(jnp.bfloat16)


def shard_levels(rng, extent, pieces, least, largest):
    def one(position, parts):
        steps = jax.random.uniform(jax.random.fold_in(jax.random.fold_in(rng, 6), position), (parts,), jnp.float32, least / len(pieces), largest / len(pieces))
        return jnp.repeat(jnp.exp(steps), extent[position] // parts).reshape((-1,) + (1,) * (len(extent) - position - 1))

    loudness = one(*pieces[0])
    for cut in pieces[1:]:
        loudness = loudness * one(*cut)
    return loudness


def profile(amount, total, limit, skew):
    loads = [(1 << 20) // math.isqrt(rank ** skew) + 1 for rank in range(2, amount + 1)]
    rest, holding = total - limit - (amount - 1), [1] * (amount - 1)
    while rest > 0:
        candidates = [i for i in range(amount - 1) if holding[i] < limit]
        mass, remaining = sum([loads[i] for i in candidates]), rest
        for i in candidates:
            extra = min(limit - holding[i], max(1, remaining * loads[i] // mass), rest)
            holding[i] = holding[i] + extra
            rest = rest - extra
    return np.array([limit] + holding)


def uneven_parts(key, amount, total, reach, skew):
    if amount == 2:
        one = jax.random.randint(key, (), max(1, total - reach), min(reach, total - 1) + 1)
        return jnp.stack([one, total - one])
    sizes = jnp.asarray(profile(amount, total, reach, skew), jnp.int32)
    pairs = (amount - 1) // 2
    giver, receiver = sizes[1:1 + 2 * pairs:2], sizes[2:2 + 2 * pairs:2]
    margin = jnp.minimum(giver - 1, reach - receiver)
    passed = jax.random.randint(jax.random.fold_in(key, 1), (pairs,), 0, 1 << 20) % (margin + 1)
    sizes = sizes.at[1:1 + 2 * pairs:2].set(giver - passed).at[2:2 + 2 * pairs:2].set(receiver + passed)
    return sizes[jax.random.permutation(jax.random.fold_in(key, 2), amount)]


def noise(own_key, shape, width, reach, cuts=(), held_as=jnp.bfloat16):
    loudness = shard_levels(own_key, shape, cuts, -0.22, 0.18) if cuts else 1.0
    array = jax.random.normal(own_key, shape, jnp.float32) * width * loudness
    return jnp.minimum(jnp.maximum(array, -reach), reach).astype(held_as)


def setup_inputs(seed: int = 0, part: int = 0) -> dict:
    seeds = jax.random.split(jax.random.key(seed), 6)
    part_splits = jax.random.split(jax.random.fold_in(seeds[5], part), 6)
    queries = draw_queries(jax.random.fold_in(jax.random.fold_in(seeds[5], part), 71), part)
    keys = draw_keys(jax.random.fold_in(jax.random.fold_in(seeds[5], part), 71), part)
    values = noise(part_splits[2], (SLAB_TOKENS, KEY_VALUE_HEADS * HEAD_SIZE), 1.0, 6.0, ((0, 8), (1, 2)))
    segments = jnp.searchsorted(jnp.cumsum(uneven_parts(part_splits[3], 8, SLAB_TOKENS, SLAB_TOKENS // 4, 2)), jnp.arange(SLAB_TOKENS), side="right").astype(jnp.int32)
    out_weight = noise(seeds[4], (QUERY_HEADS * HEAD_SIZE, D), (QUERY_HEADS * HEAD_SIZE) ** -0.5, 0.125, ((0, 2),))
    return {"queries": queries, "keys": keys, "values": values, "segments": segments, "out_weight": out_weight}


def reference(queries, keys, values, segments, out_weight):
    query_group = QUERY_HEADS // KEY_VALUE_HEADS
    token_block = math.gcd(SLAB_TOKENS, 512)
    window_span = ATTENTION_SPAN + token_block
    padded_keys = jnp.concatenate([jnp.zeros((ATTENTION_SPAN, KEY_VALUE_HEADS * HEAD_SIZE), keys.dtype), keys])
    padded_values = jnp.concatenate([jnp.zeros((ATTENTION_SPAN, KEY_VALUE_HEADS * HEAD_SIZE), values.dtype), values])
    pad_segments = jnp.concatenate([jnp.full((ATTENTION_SPAN,), -1, jnp.int32), segments.astype(jnp.int32)])

    def one_block(block_id):
        first_index = (block_id * token_block).astype(jnp.int32)
        query_matrix_rows = lax.dynamic_slice_in_dim(queries, first_index, token_block, 0).astype(jnp.float32).reshape(token_block, KEY_VALUE_HEADS, query_group, HEAD_SIZE)
        key_matrix_rows = lax.dynamic_slice_in_dim(padded_keys, first_index, window_span, 0).astype(jnp.float32).reshape(window_span, KEY_VALUE_HEADS, HEAD_SIZE)
        value_matrix_rows = lax.dynamic_slice_in_dim(padded_values, first_index, window_span, 0).astype(jnp.float32).reshape(window_span, KEY_VALUE_HEADS, HEAD_SIZE)
        seg_query = lax.dynamic_slice_in_dim(segments.astype(jnp.int32), first_index, token_block, 0)
        seg_key = lax.dynamic_slice_in_dim(pad_segments, first_index, window_span, 0)
        query_pos = first_index + jnp.arange(token_block, dtype=jnp.int32)
        key_pos = first_index - ATTENTION_SPAN + jnp.arange(window_span, dtype=jnp.int32)
        allowed = (key_pos[None, :] <= query_pos[:, None]) & (query_pos[:, None] - key_pos[None, :] < ATTENTION_SPAN) & (seg_key[None, :] == seg_query[:, None])
        scores = jnp.einsum('qkgd,pkd->kgqp', query_matrix_rows, key_matrix_rows) * (SCALAR ** -0.5)
        masked = jnp.where(allowed, scores, -1e30)
        row_max = jnp.max(masked, axis=-1, keepdims=True)
        expo = jnp.where(allowed, jnp.exp(masked - row_max), 0.0)
        weights = (expo / jnp.sum(expo, axis=-1, keepdims=True)).astype(jnp.bfloat16)
        heads_out = jnp.einsum('kgqp,pkd->qkgd', weights.astype(jnp.float32), value_matrix_rows)
        return heads_out.astype(jnp.bfloat16).reshape(token_block, QUERY_HEADS * HEAD_SIZE)

    attended = lax.map(one_block, jnp.arange(SLAB_TOKENS // token_block, dtype=jnp.int32)).reshape(SLAB_TOKENS, QUERY_HEADS * HEAD_SIZE)
    return jnp.dot(attended, out_weight, preferred_element_type=jnp.float32).astype(jnp.bfloat16)
```

```python
import jax
import jax.numpy as jnp
from jax import lax
from jax.experimental import pallas as pl
from jax.experimental.pallas import tpu as pltpu
from jax.sharding import PartitionSpec as P

HEAD_SIZE = 128
SCALAR = 168
ATTENTION_SPAN = 1024
LOG2E = 1.4426950408889634
QUERY_TILE = 256
PIECES = 2
COLUMN_STEP = 768
MESH = pl.DeviceIdType.MESH
FACTOR = SCALAR ** (-0.5) * LOG2E


def column_chunks(width):
    return [(at, min(COLUMN_STEP, width - at)) for at in range(0, width, COLUMN_STEP)]


def attend_kernel(
    q_hbm, k_hbm, v_hbm, seg_hbm, w_hbm, w_last, att_all, acc,
    w_early, seg_ref, q_s, k_s, v_s, part, part_top, bias_first, bias_near,
    own_sem, zs_sem, zr_sem, ys_sem, yr_sem, w_sem, ws_sem, wr_sem, as_sem, ar_sem,
):
    heads = att_all.shape[0]
    rows = q_s.shape[0]
    span = att_all.shape[2] // 2
    group = span // HEAD_SIZE
    width = acc.shape[1]
    tile = QUERY_TILE
    tiles = rows // tile
    size = rows // PIECES
    steps = 2 * PIECES
    seq = lax.axis_index("seq")
    core = lax.axis_index("head")
    peers = lax.axis_size("seq")
    odd = lax.rem(seq, 2)
    pair = seq + 1 - 2 * odd
    other = 1 - core
    chunks = column_chunks(width)
    has_up = seq + 2 < peers
    has_down = seq >= 2
    even = odd == 0
    sends_near = jnp.logical_or(even, seq >= 3)
    relays = jnp.logical_and(odd == 1, seq >= 3)
    takes_far = jnp.logical_and(even, has_down)
    gets_near = seq >= 1

    def head_columns(h):
        return pl.ds(pl.multiple_of(h * HEAD_SIZE, HEAD_SIZE), HEAD_SIZE)

    def piece(j):
        which, part_of = divmod(j, PIECES)
        return ((k_hbm, k_s), (v_hbm, v_s))[which], part_of * size

    def far(h, j):
        (src, dst), at = piece(j)
        return pltpu.make_async_remote_copy(
            src_ref=src.at[pl.ds(at, size), head_columns(h)],
            dst_ref=dst.at[pl.ds(at, size), head_columns(h)],
            send_sem=zs_sem.at[j // PIECES], recv_sem=zr_sem.at[h * steps + j],
            device_id={"seq": seq + 2}, device_id_type=MESH)

    def near(h, j):
        (src, dst), at = piece(j)
        return pltpu.make_async_remote_copy(
            src_ref=src.at[pl.ds(at, size), head_columns(h)],
            dst_ref=dst.at[pl.ds(2 * rows + at, size), head_columns(h)],
            send_sem=ys_sem.at[j // PIECES], recv_sem=yr_sem.at[h * steps + j],
            device_id={"seq": pair}, device_id_type=MESH)

    def relay(h, j):
        (_, dst), at = piece(j)
        return pltpu.make_async_remote_copy(
            src_ref=dst.at[pl.ds(at, size), head_columns(h)],
            dst_ref=dst.at[pl.ds(2 * rows + at, size), head_columns(h)],
            send_sem=ys_sem.at[j // PIECES], recv_sem=yr_sem.at[h * steps + j],
            device_id={"seq": pair}, device_id_type=MESH)

    def sent(which, sems, device):
        src, dst = ((k_hbm, k_s), (v_hbm, v_s))[which]
        return pltpu.make_async_remote_copy(
            src_ref=src, dst_ref=dst.at[pl.ds(0, rows), :],
            send_sem=sems.at[which], recv_sem=zr_sem.at[0],
            device_id=device, device_id_type=MESH)

    own_copies = [
        pltpu.make_async_copy(q_hbm, q_s, own_sem.at[0]),
        pltpu.make_async_copy(k_hbm, k_s.at[pl.ds(rows, rows), :], own_sem.at[1]),
        pltpu.make_async_copy(v_hbm, v_s.at[pl.ds(rows, rows), :], own_sem.at[2]),
        pltpu.make_async_copy(seg_hbm, seg_ref, own_sem.at[3]),
    ]

    own_rows = pl.ds(pl.multiple_of(core * span, span), span)
    other_rows = pl.ds(pl.multiple_of(other * span, span), span)

    def weight_rows(h):
        dst = w_last if h == heads - 1 else w_early.at[h]
        return (w_hbm.at[pl.ds(h * span, span), :],
                dst.at[own_rows, :])

    def weight_local(h):
        src, dst = weight_rows(h)
        return pltpu.make_async_copy(src, dst, w_sem.at[h])

    def weight_send(h):
        src, dst = weight_rows(h)
        return pltpu.make_async_remote_copy(
            src_ref=src, dst_ref=dst, send_sem=ws_sem.at[h], recv_sem=wr_sem.at[h],
            device_id={"head": other}, device_id_type=MESH)

    def arrived(h):
        for view, sem in ((own_rows, w_sem), (other_rows, wr_sem)):
            pltpu.make_async_copy(w_last.at[view, :], w_last.at[view, :], sem.at[h]).wait()

    def att_columns(at, count):
        return pl.ds(pl.multiple_of(core * span + at, HEAD_SIZE), count)

    def attended_send(h):
        view = att_all.at[h, :, att_columns(0, span)]
        return pltpu.make_async_remote_copy(
            src_ref=view, dst_ref=view, send_sem=as_sem.at[h], recv_sem=ar_sem.at[h],
            device_id={"head": other}, device_id_type=MESH)

    for copy in own_copies:
        copy.start()
    for h in range(heads):
        weight_local(h).start()

    barrier = pltpu.get_barrier_semaphore()
    pl.semaphore_signal(barrier, inc=1, device_id={"head": other}, device_id_type=MESH)
    pl.semaphore_signal(barrier, inc=1, device_id={"seq": pair}, device_id_type=MESH)

    @pl.when(has_up)
    def _():
        pl.semaphore_signal(barrier, inc=1, device_id={"seq": seq + 2}, device_id_type=MESH)

    @pl.when(has_down)
    def _():
        pl.semaphore_signal(barrier, inc=1, device_id={"seq": seq - 2}, device_id_type=MESH)

    pl.semaphore_wait(
        barrier, 2 + jnp.minimum(peers - 1 - seq, 2) // 2 + jnp.minimum(seq, 2) // 2)

    for h in range(heads):
        @pl.when(has_up)
        def _():
            for j in range(steps):
                far(h, j).start()

        @pl.when(even)
        def _():
            for j in range(steps):
                near(h, j).start()

        weight_send(h).start()

    @pl.when(jnp.logical_not(has_down))
    def _():
        k_s[0:rows, :] = jnp.zeros((rows, k_s.shape[1]), k_s.dtype)
        v_s[0:rows, :] = jnp.zeros((rows, v_s.shape[1]), v_s.dtype)

    @pl.when(jnp.logical_not(gets_near))
    def _():
        k_s[2 * rows:3 * rows, :] = jnp.zeros((rows, k_s.shape[1]), k_s.dtype)
        v_s[2 * rows:3 * rows, :] = jnp.zeros((rows, v_s.shape[1]), v_s.dtype)

    own_copies[3].wait()
    first = rows + tile
    seg_own = seg_ref[seq]
    seg_near = seg_ref[jnp.maximum(seq - 1, 0)] - jnp.where(gets_near, 0, 1000)
    seg_first = jnp.concatenate([seg_ref[jnp.maximum(seq - 2, 0)], seg_own], axis=1)
    for b in range(tiles):
        for sub in range(tile // 128):
            lo = b * tile + sub * 128
            here = slice(sub * 128, (sub + 1) * 128)
            seg_query = jnp.broadcast_to(
                seg_own[:, lo:lo + 128].astype(jnp.float32), (128, 128)).T[:, :1]
            r = lo + lax.broadcasted_iota(jnp.int32, (128, first), 0)
            c = b * tile + lax.broadcasted_iota(jnp.int32, (128, first), 1)
            inside = (c > r) & (c <= r + rows) & (c >= jnp.where(has_down, 0, rows))
            seg_key = seg_first[:, b * tile:b * tile + first].astype(jnp.float32)
            bias_first[b, here, :] = jnp.where(
                inside & (seg_key == seg_query), 0.0, -1e30)
            bias_near[b, here, :] = jnp.where(
                seg_near.astype(jnp.float32) == seg_query, 0.0, -1e30)
    acc[...] = jnp.zeros_like(acc)

    def with_ones(value):
        return jnp.concatenate([value, jnp.ones(value.shape, value.dtype)], axis=1)

    def score(query, key, added):
        return lax.dot_general(
            query, key, (((1,), (1,)), ((), ())), preferred_element_type=jnp.float32) + added

    def query_columns(h, g):
        return pl.ds(pl.multiple_of(h * span, HEAD_SIZE) + g * HEAD_SIZE, HEAD_SIZE)

    def first_phase(h, b):
        lines = slice(b * tile, (b + 1) * tile)
        key = k_s[b * tile:b * tile + first, head_columns(h)]
        value = with_ones(v_s[b * tile:b * tile + first, head_columns(h)])
        for g in range(group):
            scores = score(q_s[lines, query_columns(h, g)], key, bias_first[b])
            top = jnp.max(scores, axis=1, keepdims=True)
            weights = jnp.exp2((scores - top) * FACTOR).astype(jnp.bfloat16)
            part[g, lines, :] = jnp.dot(weights, value, preferred_element_type=jnp.float32)
            part_top[g, lines, :] = jnp.broadcast_to(top, (tile, HEAD_SIZE))

    def near_phase(h, b):
        lines = slice(b * tile, (b + 1) * tile)
        key = k_s[2 * rows:3 * rows, head_columns(h)]
        value = with_ones(v_s[2 * rows:3 * rows, head_columns(h)])
        for g in range(group):
            scores = score(q_s[lines, query_columns(h, g)], key, bias_near[b])
            before = part_top[g, lines, :]
            top = jnp.maximum(jnp.max(scores, axis=1, keepdims=True), before[:, :1])
            weights = jnp.exp2((scores - top) * FACTOR).astype(jnp.bfloat16)
            faded = jnp.exp2((before - top) * FACTOR)
            mix = part[g, lines, :] * jnp.concatenate([faded, faded], axis=1) + jnp.dot(
                weights, value, preferred_element_type=jnp.float32)
            att_all[h, lines, att_columns(g * HEAD_SIZE, HEAD_SIZE)] = (
                mix[:, :HEAD_SIZE] / mix[:, HEAD_SIZE:]).astype(jnp.bfloat16)

    def forward(h, j, wanted):
        @pl.when(jnp.logical_and(relays, wanted))
        def _():
            far(h, j).wait_recv()
            relay(h, j).start()

    for copy in own_copies[:3]:
        copy.wait()
    for j in range(steps):
        forward(0, j, True)

    def step(h, carry):
        more = h + 1 < heads

        def product(some):
            for at, count in some:
                acc[:, at:at + count] += jnp.dot(
                    att_all[h - 1], w_early[h - 1, :, at:at + count],
                    preferred_element_type=jnp.float32)

        @pl.when(takes_far)
        def _():
            for j in range(steps):
                far(h, j).wait_recv()

        for b in range(tiles):
            first_phase(h, b)
        forward(h + 1, 0, more)

        @pl.when(gets_near)
        def _():
            for j in range(steps):
                near(h, j).wait_recv()

        for b in range(tiles):
            near_phase(h, b)
        attended_send(h).start()

        @pl.when(h >= 1)
        def _():
            attended_send(h - 1).wait_recv()
            arrived(h - 1)
            product(chunks[:2])
        forward(h + 1, 1, more)

        @pl.when(h >= 1)
        def _():
            product(chunks[2:5])
        forward(h + 1, 2, more)

        @pl.when(h >= 1)
        def _():
            product(chunks[5:])
        forward(h + 1, 3, more)
        return carry

    lax.fori_loop(0, heads, step, 0)

    arrived(heads - 1)
    for which in range(2):
        @pl.when(has_up)
        def _():
            sent(which, zs_sem, {"seq": seq + 2}).wait_send()

        @pl.when(sends_near)
        def _():
            sent(which, ys_sem, {"seq": pair}).wait_send()
    for h in range(heads):
        weight_send(h).wait_send()
        attended_send(h).wait_send()
    attended_send(heads - 1).wait_recv()


def finish_kernel(w_last, att_all, acc, out_hbm, out_s, sem):
    last = att_all.shape[0] - 1
    copies = []
    for n, (at, count) in enumerate(column_chunks(acc.shape[1])):
        out_s[:, at:at + count] = (acc[:, at:at + count] + jnp.dot(
            att_all[last], w_last[:, at:at + count],
            preferred_element_type=jnp.float32)).astype(jnp.bfloat16)
        copy = pltpu.make_async_copy(
            out_s.at[:, pl.ds(at, count)], out_hbm.at[:, pl.ds(at, count)], sem.at[n])
        copy.start()
        copies.append(copy)
    for copy in copies:
        copy.wait()


def shards(queries, keys, values, segments, out_weight):
    rows = queries.shape[0]
    assert 2 * rows == ATTENTION_SPAN
    heads = keys.shape[1] // HEAD_SIZE
    query_heads = queries.shape[1] // HEAD_SIZE
    span = query_heads // heads * HEAD_SIZE
    group = query_heads // heads
    width = out_weight.shape[1]
    tiles = rows // QUERY_TILE
    seg = segments.reshape(segments.shape[0] // rows, 1, rows)
    dma = pltpu.SemaphoreType.DMA
    anywhere = pl.BlockSpec(memory_space=pltpu.HBM)
    here = pl.BlockSpec(memory_space=pltpu.VMEM)
    bf16, f32 = jnp.bfloat16, jnp.float32
    pieces = heads * 2 * PIECES
    w_last, att_all, acc = pl.pallas_call(
        attend_kernel,
        out_shape=(
            pltpu.VMEM((2 * span, width), bf16),
            pltpu.VMEM((heads, rows, 2 * span), bf16),
            pltpu.VMEM((rows, width), f32),
        ),
        in_specs=[anywhere] * 5,
        out_specs=(here, here, here),
        scratch_shapes=[
            pltpu.VMEM((heads - 1, 2 * span, width), bf16),
            pltpu.VMEM(seg.shape, seg.dtype),
            pltpu.VMEM(queries.shape, bf16),
            pltpu.VMEM((3 * rows, keys.shape[1]), bf16),
            pltpu.VMEM((3 * rows, keys.shape[1]), bf16),
            pltpu.VMEM((group, rows, 2 * HEAD_SIZE), f32),
            pltpu.VMEM((group, rows, HEAD_SIZE), f32),
            pltpu.VMEM((tiles, QUERY_TILE, rows + QUERY_TILE), f32),
            pltpu.VMEM((tiles, QUERY_TILE, rows), f32),
            dma((4,)), dma((2,)), dma((pieces,)), dma((2,)), dma((pieces,)),
            dma((heads,)), dma((heads,)), dma((heads,)), dma((heads,)), dma((heads,)),
        ],
        compiler_params=pltpu.CompilerParams(
            collective_id=0, has_side_effects=True, vmem_limit_bytes=36 * 1024 * 1024),
    )(queries, keys, values, pltpu.with_memory_space_constraint(seg, pltpu.HBM), out_weight)
    return pl.pallas_call(
        finish_kernel,
        out_shape=jax.ShapeDtypeStruct((rows, width), bf16),
        in_specs=[here, here, here],
        out_specs=anywhere,
        scratch_shapes=[
            pltpu.VMEM((rows, width), bf16), dma((len(column_chunks(width)),)),
        ],
        compiler_params=pltpu.CompilerParams(vmem_limit_bytes=16 * 1024 * 1024),
    )(w_last, att_all, acc)


def solution(mesh):
    placed = (
        P(("groups", "seq"), "head"),
        P(("groups", "seq"), "head"),
        P(("groups", "seq"), "head"),
        P("groups"),
        P("head", None),
    )
    return jax.shard_map(
        shards, mesh=mesh, in_specs=placed, out_specs=P(("groups", "seq"), None), check_vma=False
    )
```

```python
import jax
import jax.numpy as jnp
from jax import lax
from jax.experimental import pallas as pl
from jax.experimental.pallas import tpu as pltpu
from jax.sharding import PartitionSpec as P

HEAD_SIZE = 128
SCALAR = 168
ATTENTION_SPAN = 1024
LOG2E = 1.4426950408889634
QUERY_TILE = 256
PIECES = 2
COLUMN_STEP = 768
MESH = pl.DeviceIdType.MESH
FACTOR = SCALAR ** (-0.5) * LOG2E


def column_chunks(width):
    return [(at, min(COLUMN_STEP, width - at)) for at in range(0, width, COLUMN_STEP)]


def attend_kernel(
    q_hbm, k_hbm, v_hbm, seg_hbm, w_hbm, w_last, att_all, early, mine,
    w_early, acc, seg_ref, q_s, k_s, v_s, part, part_top, probs, bias,
    own_sem, zs_sem, zr_sem, ys_sem, yr_sem, w_sem, ws_sem, wr_sem, as_sem, ar_sem, es_sem, er_sem,
):
    heads = att_all.shape[0]
    rows = q_s.shape[0]
    span = att_all.shape[2] // 2
    group = span // HEAD_SIZE
    width = mine.shape[1]
    half = acc.shape[1]
    tile = QUERY_TILE
    tiles = rows // tile
    size = rows // PIECES
    steps = 2 * PIECES
    seq = lax.axis_index("seq")
    core = lax.axis_index("head")
    peers = lax.axis_size("seq")
    odd = lax.rem(seq, 2)
    pair = seq + 1 - 2 * odd
    other = 1 - core
    chunks = column_chunks(half)
    has_up = seq + 2 < peers
    has_down = seq >= 2
    even = odd == 0
    sends_near = jnp.logical_or(even, seq >= 3)
    relays = jnp.logical_and(odd == 1, seq >= 3)
    takes_far = jnp.logical_and(even, has_down)
    gets_near = seq >= 1

    def head_columns(h):
        return pl.ds(pl.multiple_of(h * HEAD_SIZE, HEAD_SIZE), HEAD_SIZE)

    def piece(j):
        which, part_of = divmod(j, PIECES)
        return ((k_hbm, k_s), (v_hbm, v_s))[which], part_of * size

    def far(h, j):
        (src, dst), at = piece(j)
        return pltpu.make_async_remote_copy(
            src_ref=src.at[pl.ds(at, size), head_columns(h)],
            dst_ref=dst.at[pl.ds(at, size), head_columns(h)],
            send_sem=zs_sem.at[j // PIECES], recv_sem=zr_sem.at[h * steps + j],
            device_id={"seq": seq + 2}, device_id_type=MESH)

    def near(h, j):
        (src, dst), at = piece(j)
        return pltpu.make_async_remote_copy(
            src_ref=src.at[pl.ds(at, size), head_columns(h)],
            dst_ref=dst.at[pl.ds(rows + at, size), head_columns(h)],
            send_sem=ys_sem.at[j // PIECES], recv_sem=yr_sem.at[2 * h + j // PIECES],
            device_id={"seq": pair}, device_id_type=MESH)

    def relay(h, j):
        (_, dst), at = piece(j)
        return pltpu.make_async_remote_copy(
            src_ref=dst.at[pl.ds(at, size), head_columns(h)],
            dst_ref=dst.at[pl.ds(rows + at, size), head_columns(h)],
            send_sem=ys_sem.at[j // PIECES], recv_sem=yr_sem.at[2 * h + j // PIECES],
            device_id={"seq": pair}, device_id_type=MESH)

    def sent(which, sems, device):
        src, dst = ((k_hbm, k_s), (v_hbm, v_s))[which]
        return pltpu.make_async_remote_copy(
            src_ref=src, dst_ref=dst.at[pl.ds(0, rows), :],
            send_sem=sems.at[which], recv_sem=zr_sem.at[0],
            device_id=device, device_id_type=MESH)

    own_copies = [
        pltpu.make_async_copy(q_hbm, q_s, own_sem.at[0]),
        pltpu.make_async_copy(k_hbm, k_s.at[pl.ds(2 * rows, rows), :], own_sem.at[1]),
        pltpu.make_async_copy(v_hbm, v_s.at[pl.ds(2 * rows, rows), :], own_sem.at[2]),
        pltpu.make_async_copy(seg_hbm, seg_ref, own_sem.at[3]),
    ]

    own_rows = pl.ds(pl.multiple_of(core * span, span), span)
    other_rows = pl.ds(pl.multiple_of(other * span, span), span)

    def half_columns(which, at, count):
        return pl.ds(pl.multiple_of(which * half + at, HEAD_SIZE), count)

    def weight_copy(h, whose):
        src = w_hbm.at[pl.ds(h * span, span)]
        if h == heads - 1:
            return src, w_last.at[own_rows]
        return src.at[:, half_columns(whose, 0, half)], w_early.at[h, own_rows]

    def weight_local(h):
        src, dst = weight_copy(h, core)
        return pltpu.make_async_copy(src, dst, w_sem.at[h])

    def weight_send(h):
        src, dst = weight_copy(h, other)
        return pltpu.make_async_remote_copy(
            src_ref=src, dst_ref=dst, send_sem=ws_sem.at[h], recv_sem=wr_sem.at[h],
            device_id={"head": other}, device_id_type=MESH)

    def early_send(at, count):
        view = early.at[:, half_columns(core, at, count)]
        return pltpu.make_async_remote_copy(
            src_ref=view, dst_ref=view, send_sem=es_sem, recv_sem=er_sem,
            device_id={"head": other}, device_id_type=MESH)

    def att_columns(at, count):
        return pl.ds(pl.multiple_of(core * span + at, HEAD_SIZE), count)

    def attended_send(h):
        view = att_all.at[h, :, att_columns(0, span)]
        return pltpu.make_async_remote_copy(
            src_ref=view, dst_ref=view, send_sem=as_sem, recv_sem=ar_sem.at[h],
            device_id={"head": other}, device_id_type=MESH)

    for copy in own_copies:
        copy.start()
    for h in range(heads):
        weight_local(h).start()

    barrier = pltpu.get_barrier_semaphore()
    pl.semaphore_signal(barrier, inc=1, device_id={"head": other}, device_id_type=MESH)
    pl.semaphore_signal(barrier, inc=1, device_id={"seq": pair}, device_id_type=MESH)

    @pl.when(has_up)
    def _():
        pl.semaphore_signal(barrier, inc=1, device_id={"seq": seq + 2}, device_id_type=MESH)

    @pl.when(has_down)
    def _():
        pl.semaphore_signal(barrier, inc=1, device_id={"seq": seq - 2}, device_id_type=MESH)

    pl.semaphore_wait(
        barrier, 2 + jnp.minimum(peers - 1 - seq, 2) // 2 + jnp.minimum(seq, 2) // 2)

    for h in range(heads):
        @pl.when(has_up)
        def _():
            for j in range(steps):
                far(h, j).start()

        @pl.when(even)
        def _():
            for j in range(steps):
                near(h, j).start()

        weight_send(h).start()

    @pl.when(jnp.logical_not(has_down))
    def _():
        k_s[0:rows, :] = jnp.zeros((rows, k_s.shape[1]), k_s.dtype)
        v_s[0:rows, :] = jnp.zeros((rows, v_s.shape[1]), v_s.dtype)

    @pl.when(jnp.logical_not(gets_near))
    def _():
        k_s[rows:2 * rows, :] = jnp.zeros((rows, k_s.shape[1]), k_s.dtype)
        v_s[rows:2 * rows, :] = jnp.zeros((rows, v_s.shape[1]), v_s.dtype)

    own_copies[3].wait()
    span_all = 3 * rows
    seg_own = seg_ref[seq]
    seg_keys = jnp.concatenate([
        seg_ref[jnp.maximum(seq - 2, 0)] - jnp.where(has_down, 0, 1000),
        seg_ref[jnp.maximum(seq - 1, 0)] - jnp.where(gets_near, 0, 1000),
        seg_own,
    ], axis=1).astype(jnp.float32)
    for n in range(rows // 128):
        here = slice(n * 128, (n + 1) * 128)
        seg_query = jnp.broadcast_to(
            seg_own[:, here].astype(jnp.float32), (128, 128)).T[:, :1]
        r = n * 128 + lax.broadcasted_iota(jnp.int32, (128, span_all), 0)
        c = lax.broadcasted_iota(jnp.int32, (128, span_all), 1)
        inside = (c > r) & (c <= r + 2 * rows)
        bias[here, :] = jnp.where(inside & (seg_keys == seg_query), 0.0, -1e30)
    acc[...] = jnp.zeros_like(acc)

    def with_ones(value):
        return jnp.concatenate([value, jnp.ones(value.shape, value.dtype)], axis=1)

    def query_columns(h, g):
        return pl.ds(pl.multiple_of(h * span, HEAD_SIZE) + g * HEAD_SIZE, HEAD_SIZE)

    halo = 2 * rows

    def score(h, g, lines, keys):
        return lax.dot_general(
            q_s[lines, query_columns(h, g)], k_s[keys, head_columns(h)],
            (((1,), (1,)), ((), ())), preferred_element_type=jnp.float32) + bias[lines, keys]

    def own_phase(h, b):
        lines, keys = slice(b * tile, (b + 1) * tile), slice(halo, halo + (b + 1) * tile)
        value = with_ones(v_s[keys, head_columns(h)])
        for g in range(group):
            n = h * group + g
            scores = score(h, g, lines, keys)
            top = jnp.max(scores, axis=1, keepdims=True)
            weights = jnp.exp2((scores - top) * FACTOR).astype(jnp.bfloat16)
            part[n, lines, :] = jnp.dot(weights, value, preferred_element_type=jnp.float32)
            part_top[n, lines, :] = jnp.broadcast_to(top, (tile, HEAD_SIZE))

    def halo_weights(h, b):
        lines, keys = slice(b * tile, (b + 1) * tile), slice(b * tile, halo)
        for g in range(group):
            n = h * group + g
            scores = score(h, g, lines, keys)
            before = part_top[n, lines, :]
            top = jnp.maximum(jnp.max(scores, axis=1, keepdims=True), before[:, :1])
            probs[g, lines, keys] = jnp.exp2((scores - top) * FACTOR).astype(jnp.bfloat16)
            part_top[n, lines, :] = jnp.exp2((before - top) * FACTOR)

    def halo_values(h, b):
        lines, keys = slice(b * tile, (b + 1) * tile), slice(b * tile, halo)
        value = with_ones(v_s[keys, head_columns(h)])
        for g in range(group):
            n = h * group + g
            faded = part_top[n, lines, :]
            mix = part[n, lines, :] * jnp.concatenate([faded, faded], axis=1) + jnp.dot(
                probs[g, lines, keys], value, preferred_element_type=jnp.float32)
            att_all[h, lines, att_columns(g * HEAD_SIZE, HEAD_SIZE)] = (
                mix[:, :HEAD_SIZE] / mix[:, HEAD_SIZE:]).astype(jnp.bfloat16)

    def forward(h, j):
        @pl.when(relays)
        def _():
            far(h, j).wait_recv()
            relay(h, j).start()

    for copy in own_copies[:3]:
        copy.wait()

    def own_step(h, carry):
        for b in range(tiles):
            own_phase(h, b)
        return carry

    lax.fori_loop(0, heads // 2, own_step, 0)
    forward(0, 0)
    lax.fori_loop(heads // 2, heads, own_step, 0)

    def step(h, carry):
        def product(some):
            @pl.when(h >= 1)
            def _():
                for at, count in some:
                    acc[:, at:at + count] += jnp.dot(
                        att_all[h - 1], w_early[h - 1, :, at:at + count],
                        preferred_element_type=jnp.float32)

            @pl.when(h == heads - 1)
            def _():
                for at, count in some:
                    early[:, half_columns(core, at, count)] = (
                        acc[:, at:at + count].astype(jnp.bfloat16))
                    early_send(at, count).start()

        @pl.when(h >= 1)
        def _():
            forward(h, 0)
            attended_send(h - 1).wait_recv()
            for rows_of, sem in ((own_rows, w_sem), (other_rows, wr_sem)):
                view = w_early.at[h - 1, rows_of]
                pltpu.make_async_copy(view, view, sem.at[h - 1]).wait()

        def halo_there(h, which):
            @pl.when(takes_far)
            def _():
                for j in range(which * PIECES, (which + 1) * PIECES):
                    far(h, j).wait_recv()

            @pl.when(gets_near)
            def _():
                view = (k_s, v_s)[which].at[pl.ds(rows, rows), head_columns(h)]
                pltpu.make_async_copy(view, view, yr_sem.at[2 * h + which]).wait()

        product(chunks[:1])
        forward(h, 1)
        halo_there(h, 0)
        for b in range(tiles):
            halo_weights(h, b)
        product(chunks[1:2])
        forward(h, 2)
        product(chunks[2:])
        forward(h, 3)
        halo_there(h, 1)
        for b in range(tiles):
            halo_values(h, b)
        attended_send(h).start()
        return carry

    lax.fori_loop(0, heads, step, 0)

    weight_local(heads - 1).wait()
    weight_send(heads - 1).wait_recv()
    for at, count in column_chunks(width):
        mine[:, at:at + count] = jnp.dot(
            att_all[heads - 1, :, att_columns(0, span)], w_last[own_rows, at:at + count],
            preferred_element_type=jnp.float32)

    for which in range(2):
        @pl.when(has_up)
        def _():
            sent(which, zs_sem, {"seq": seq + 2}).wait_send()

        @pl.when(sends_near)
        def _():
            sent(which, ys_sem, {"seq": pair}).wait_send()
    for h in range(heads):
        weight_send(h).wait_send()
    for whose, sem in ((core, es_sem), (other, er_sem)):
        view = early.at[:, half_columns(whose, 0, half)]
        pltpu.make_async_copy(view, view, sem).wait()
    pltpu.make_async_copy(
        att_all.at[:, :, att_columns(0, span)], att_all.at[:, :, att_columns(0, span)], as_sem).wait()
    attended_send(heads - 1).wait_recv()


def finish_kernel(w_last, att_all, early, mine, out_hbm, out_s, sem):
    last = att_all.shape[0] - 1
    span = att_all.shape[2] // 2
    theirs = pl.ds(pl.multiple_of((1 - lax.axis_index("head")) * span, span), span)
    copies = []
    for n, (at, count) in enumerate(column_chunks(mine.shape[1])):
        here = slice(at, at + count)
        out_s[:, here] = (early[:, here].astype(jnp.float32) + (mine[:, here] + jnp.dot(
            att_all[last, :, theirs], w_last[theirs, here],
            preferred_element_type=jnp.float32))).astype(jnp.bfloat16)
        copy = pltpu.make_async_copy(
            out_s.at[:, pl.ds(at, count)], out_hbm.at[:, pl.ds(at, count)], sem.at[n])
        copy.start()
        copies.append(copy)
    for copy in copies:
        copy.wait()


def shards(queries, keys, values, segments, out_weight):
    rows = queries.shape[0]
    assert 2 * rows == ATTENTION_SPAN
    heads = keys.shape[1] // HEAD_SIZE
    query_heads = queries.shape[1] // HEAD_SIZE
    span = query_heads // heads * HEAD_SIZE
    width = out_weight.shape[1]
    seg = segments.reshape(segments.shape[0] // rows, 1, rows)
    dma = pltpu.SemaphoreType.DMA
    anywhere = pl.BlockSpec(memory_space=pltpu.HBM)
    here = pl.BlockSpec(memory_space=pltpu.VMEM)
    bf16, f32 = jnp.bfloat16, jnp.float32
    pieces = heads * 2 * PIECES
    w_last, att_all, early, mine = pl.pallas_call(
        attend_kernel,
        out_shape=(
            pltpu.VMEM((2 * span, width), bf16),
            pltpu.VMEM((heads, rows, 2 * span), bf16),
            pltpu.VMEM((rows, width), bf16),
            pltpu.VMEM((rows, width), f32),
        ),
        in_specs=[anywhere] * 5,
        out_specs=(here,) * 4,
        scratch_shapes=[
            pltpu.VMEM((heads - 1, 2 * span, width // 2), bf16),
            pltpu.VMEM((rows, width // 2), f32),
            pltpu.VMEM(seg.shape, seg.dtype),
            pltpu.VMEM(queries.shape, bf16),
            pltpu.VMEM((3 * rows, keys.shape[1]), bf16),
            pltpu.VMEM((3 * rows, keys.shape[1]), bf16),
            pltpu.VMEM((query_heads, rows, 2 * HEAD_SIZE), f32),
            pltpu.VMEM((query_heads, rows, HEAD_SIZE), f32),
            pltpu.VMEM((query_heads // heads, rows, 2 * rows), bf16),
            pltpu.VMEM((rows, 3 * rows), f32),
            dma((4,)), dma((2,)), dma((pieces,)), dma((2,)), dma((2 * heads,)),
            dma((heads,)), dma((heads,)), dma((heads,)), dma, dma((heads,)), dma, dma,
        ],
        compiler_params=pltpu.CompilerParams(
            collective_id=0, has_side_effects=True, vmem_limit_bytes=34 * 1024 * 1024),
    )(queries, keys, values, pltpu.with_memory_space_constraint(seg, pltpu.HBM), out_weight)
    return pl.pallas_call(
        finish_kernel,
        out_shape=jax.ShapeDtypeStruct((rows, width), bf16),
        in_specs=[here] * 4,
        out_specs=anywhere,
        scratch_shapes=[
            pltpu.VMEM((rows, width), bf16), dma((len(column_chunks(width)),)),
        ],
        compiler_params=pltpu.CompilerParams(vmem_limit_bytes=12 * 1024 * 1024),
    )(w_last, att_all, early, mine)


def solution(mesh):
    placed = (
        P(("groups", "seq"), "head"),
        P(("groups", "seq"), "head"),
        P(("groups", "seq"), "head"),
        P("groups"),
        P("head", None),
    )
    return jax.shard_map(
        shards, mesh=mesh, in_specs=placed, out_specs=P(("groups", "seq"), None), check_vma=False
    )
```

```python
import jax
import jax.numpy as jnp
from jax import lax
from jax.experimental import pallas as pl
from jax.experimental.pallas import tpu as pltpu
from jax.sharding import PartitionSpec as P

HEAD_SIZE = 128
SCALAR = 168
ATTENTION_SPAN = 1024
LOG2E = 1.4426950408889634
QUERY_TILE = 256
PIECES = 2
COLUMN_STEP = 768
MESH = pl.DeviceIdType.MESH
FACTOR = SCALAR ** (-0.5) * LOG2E


def column_chunks(width):
    return [(at, min(COLUMN_STEP, width - at)) for at in range(0, width, COLUMN_STEP)]


def attend_kernel(
    q_hbm, k_hbm, v_hbm, seg_hbm, w_hbm, w_last, att_all, early, mine,
    w_early, acc, seg_ref, q_s, k_s, v_s, part, part_top, probs, bias,
    own_sem, zs_sem, zr_sem, ys_sem, yr_sem, w_sem, ws_sem, wr_sem, as_sem, ar_sem, es_sem, er_sem,
):
    heads = att_all.shape[0]
    rows = q_s.shape[0]
    span = att_all.shape[2] // 2
    group = span // HEAD_SIZE
    width = mine.shape[1]
    half = acc.shape[1]
    tile = QUERY_TILE
    tiles = rows // tile
    size = rows // PIECES
    steps = 2 * PIECES
    seq = lax.axis_index("seq")
    core = lax.axis_index("head")
    peers = lax.axis_size("seq")
    odd = lax.rem(seq, 2)
    pair = seq + 1 - 2 * odd
    other = 1 - core
    chunks = column_chunks(half)
    has_up = seq + 2 < peers
    has_down = seq >= 2
    even = odd == 0
    sends_near = jnp.logical_or(even, seq >= 3)
    relays = jnp.logical_and(odd == 1, seq >= 3)
    takes_far = jnp.logical_and(even, has_down)
    gets_near = seq >= 1

    def head_columns(h):
        return pl.ds(pl.multiple_of(h * HEAD_SIZE, HEAD_SIZE), HEAD_SIZE)

    def piece(j):
        which, part_of = divmod(j, PIECES)
        return ((k_hbm, k_s), (v_hbm, v_s))[which], part_of * size

    def far(h, j):
        (src, dst), at = piece(j)
        return pltpu.make_async_remote_copy(
            src_ref=src.at[pl.ds(at, size), head_columns(h)],
            dst_ref=dst.at[pl.ds(at, size), head_columns(h)],
            send_sem=zs_sem.at[j // PIECES], recv_sem=zr_sem.at[h * steps + j],
            device_id={"seq": seq + 2}, device_id_type=MESH)

    def near(h, j):
        (src, dst), at = piece(j)
        return pltpu.make_async_remote_copy(
            src_ref=src.at[pl.ds(at, size), head_columns(h)],
            dst_ref=dst.at[pl.ds(rows + at, size), head_columns(h)],
            send_sem=ys_sem.at[j // PIECES], recv_sem=yr_sem.at[2 * h + j // PIECES],
            device_id={"seq": pair}, device_id_type=MESH)

    def relay(h, j):
        (_, dst), at = piece(j)
        return pltpu.make_async_remote_copy(
            src_ref=dst.at[pl.ds(at, size), head_columns(h)],
            dst_ref=dst.at[pl.ds(rows + at, size), head_columns(h)],
            send_sem=ys_sem.at[j // PIECES], recv_sem=yr_sem.at[2 * h + j // PIECES],
            device_id={"seq": pair}, device_id_type=MESH)

    def sent(which, sems, device):
        src, dst = ((k_hbm, k_s), (v_hbm, v_s))[which]
        return pltpu.make_async_remote_copy(
            src_ref=src, dst_ref=dst.at[pl.ds(0, rows), :],
            send_sem=sems.at[which], recv_sem=zr_sem.at[0],
            device_id=device, device_id_type=MESH)

    own_copies = [
        pltpu.make_async_copy(q_hbm, q_s, own_sem.at[0]),
        pltpu.make_async_copy(k_hbm, k_s.at[pl.ds(2 * rows, rows), :], own_sem.at[1]),
        pltpu.make_async_copy(v_hbm, v_s.at[pl.ds(2 * rows, rows), :], own_sem.at[2]),
        pltpu.make_async_copy(seg_hbm, seg_ref, own_sem.at[3]),
    ]

    own_rows = pl.ds(pl.multiple_of(core * span, span), span)
    other_rows = pl.ds(pl.multiple_of(other * span, span), span)

    def half_columns(which, at, count):
        return pl.ds(pl.multiple_of(which * half + at, HEAD_SIZE), count)

    def weight_copy(h, whose):
        src = w_hbm.at[pl.ds(h * span, span)]
        if h == heads - 1:
            return src, w_last.at[own_rows]
        return src.at[:, half_columns(whose, 0, half)], w_early.at[h, own_rows]

    def weight_local(h):
        src, dst = weight_copy(h, core)
        return pltpu.make_async_copy(src, dst, w_sem.at[h])

    def weight_send(h):
        src, dst = weight_copy(h, other)
        return pltpu.make_async_remote_copy(
            src_ref=src, dst_ref=dst, send_sem=ws_sem.at[h], recv_sem=wr_sem.at[h],
            device_id={"head": other}, device_id_type=MESH)

    def early_send(at, count):
        view = early.at[:, half_columns(core, at, count)]
        return pltpu.make_async_remote_copy(
            src_ref=view, dst_ref=view, send_sem=es_sem, recv_sem=er_sem,
            device_id={"head": other}, device_id_type=MESH)

    def att_columns(at, count):
        return pl.ds(pl.multiple_of(core * span + at, HEAD_SIZE), count)

    def attended_send(h):
        view = att_all.at[h, :, att_columns(0, span)]
        return pltpu.make_async_remote_copy(
            src_ref=view, dst_ref=view, send_sem=as_sem, recv_sem=ar_sem.at[h],
            device_id={"head": other}, device_id_type=MESH)

    for copy in own_copies:
        copy.start()
    for h in range(heads):
        weight_local(h).start()

    barrier = pltpu.get_barrier_semaphore()
    pl.semaphore_signal(barrier, inc=1, device_id={"head": other}, device_id_type=MESH)
    pl.semaphore_signal(barrier, inc=1, device_id={"seq": pair}, device_id_type=MESH)

    @pl.when(has_up)
    def _():
        pl.semaphore_signal(barrier, inc=1, device_id={"seq": seq + 2}, device_id_type=MESH)

    @pl.when(has_down)
    def _():
        pl.semaphore_signal(barrier, inc=1, device_id={"seq": seq - 2}, device_id_type=MESH)

    pl.semaphore_wait(
        barrier, 2 + jnp.minimum(peers - 1 - seq, 2) // 2 + jnp.minimum(seq, 2) // 2)

    for h in range(heads):
        @pl.when(has_up)
        def _():
            for j in range(steps):
                far(h, j).start()

        @pl.when(even)
        def _():
            for j in range(steps):
                near(h, j).start()

        weight_send(h).start()

    @pl.when(jnp.logical_not(has_down))
    def _():
        k_s[0:rows, :] = jnp.zeros((rows, k_s.shape[1]), k_s.dtype)
        v_s[0:rows, :] = jnp.zeros((rows, v_s.shape[1]), v_s.dtype)

    @pl.when(jnp.logical_not(gets_near))
    def _():
        k_s[rows:2 * rows, :] = jnp.zeros((rows, k_s.shape[1]), k_s.dtype)
        v_s[rows:2 * rows, :] = jnp.zeros((rows, v_s.shape[1]), v_s.dtype)

    own_copies[3].wait()
    span_all = 3 * rows
    seg_own = seg_ref[seq]
    seg_keys = jnp.concatenate([
        seg_ref[jnp.maximum(seq - 2, 0)] - jnp.where(has_down, 0, 1000),
        seg_ref[jnp.maximum(seq - 1, 0)] - jnp.where(gets_near, 0, 1000),
        seg_own,
    ], axis=1).astype(jnp.float32)
    for n in range(rows // 128):
        here = slice(n * 128, (n + 1) * 128)
        seg_query = jnp.broadcast_to(
            seg_own[:, here].astype(jnp.float32), (128, 128)).T[:, :1]
        r = n * 128 + lax.broadcasted_iota(jnp.int32, (128, span_all), 0)
        c = lax.broadcasted_iota(jnp.int32, (128, span_all), 1)
        inside = (c > r) & (c <= r + 2 * rows)
        bias[here, :] = jnp.where(inside & (seg_keys == seg_query), 0.0, -1e30)
    acc[...] = jnp.zeros_like(acc)

    def with_ones(value):
        return jnp.concatenate([value, jnp.ones(value.shape, value.dtype)], axis=1)

    def query_columns(h, g):
        return pl.ds(pl.multiple_of(h * span, HEAD_SIZE) + g * HEAD_SIZE, HEAD_SIZE)

    halo = 2 * rows

    def score(h, g, lines, keys):
        return lax.dot_general(
            q_s[lines, query_columns(h, g)], k_s[keys, head_columns(h)],
            (((1,), (1,)), ((), ())), preferred_element_type=jnp.float32) + bias[lines, keys]

    def own_phase(h, b):
        lines, keys = slice(b * tile, (b + 1) * tile), slice(halo, halo + (b + 1) * tile)
        value = with_ones(v_s[keys, head_columns(h)])
        for g in range(group):
            n = h * group + g
            scores = score(h, g, lines, keys)
            top = jnp.max(scores, axis=1, keepdims=True)
            weights = jnp.exp2((scores - top) * FACTOR).astype(jnp.bfloat16)
            part[n, lines, :] = jnp.dot(weights, value, preferred_element_type=jnp.float32)
            part_top[n, lines, :] = jnp.broadcast_to(top, (tile, HEAD_SIZE))

    def halo_weights(h, b):
        lines, keys = slice(b * tile, (b + 1) * tile), slice(b * tile, halo)
        for g in range(group):
            n = h * group + g
            scores = score(h, g, lines, keys)
            before = part_top[n, lines, :]
            top = jnp.maximum(jnp.max(scores, axis=1, keepdims=True), before[:, :1])
            probs[g, lines, keys] = jnp.exp2((scores - top) * FACTOR).astype(jnp.bfloat16)
            part_top[n, lines, :] = jnp.exp2((before - top) * FACTOR)

    def halo_values(h, b):
        lines, keys = slice(b * tile, (b + 1) * tile), slice(b * tile, halo)
        value = with_ones(v_s[keys, head_columns(h)])
        for g in range(group):
            n = h * group + g
            faded = part_top[n, lines, :]
            mix = part[n, lines, :] * jnp.concatenate([faded, faded], axis=1) + jnp.dot(
                probs[g, lines, keys], value, preferred_element_type=jnp.float32)
            att_all[h, lines, att_columns(g * HEAD_SIZE, HEAD_SIZE)] = (
                mix[:, :HEAD_SIZE] / mix[:, HEAD_SIZE:]).astype(jnp.bfloat16)

    def forward(h, j):
        @pl.when(relays)
        def _():
            far(h, j).wait_recv()
            relay(h, j).start()

    for copy in own_copies[:3]:
        copy.wait()

    def own_step(h, carry):
        for b in range(tiles):
            own_phase(h, b)
        for j, after in ((0, 0), (1, 1), (2, heads - 1)):
            @pl.when(h == after)
            def _():
                forward(0, j)
        return carry

    lax.fori_loop(0, heads, own_step, 0)

    def halo_there(h, which):
        @pl.when(takes_far)
        def _():
            for j in range(which * PIECES, (which + 1) * PIECES):
                far(h, j).wait_recv()

        @pl.when(gets_near)
        def _():
            view = (k_s, v_s)[which].at[pl.ds(rows, rows), head_columns(h)]
            pltpu.make_async_copy(view, view, yr_sem.at[2 * h + which]).wait()

    def attend(h):
        halo_there(h, 1)
        for b in range(tiles):
            halo_values(h, b)
        attended_send(h).start()

    def step(h, carry):
        def product(some):
            for at, count in some:
                acc[:, at:at + count] += jnp.dot(
                    att_all[h - 1], w_early[h - 1, :, at:at + count],
                    preferred_element_type=jnp.float32)

            @pl.when(h == heads - 1)
            def _():
                for at, count in some:
                    early[:, half_columns(core, at, count)] = (
                        acc[:, at:at + count].astype(jnp.bfloat16))
                    early_send(at, count).start()

        @pl.when(h >= 1)
        def _():
            forward(h, 0)
            attend(h - 1)
            forward(h, 1)
            attended_send(h - 1).wait_recv()
            for rows_of, sem in ((own_rows, w_sem), (other_rows, wr_sem)):
                view = w_early.at[h - 1, rows_of]
                pltpu.make_async_copy(view, view, sem.at[h - 1]).wait()
            product(chunks[:2])
            forward(h, 2)
            product(chunks[2:])

        forward(h, 3)
        halo_there(h, 0)
        for b in range(tiles):
            halo_weights(h, b)
        return carry

    lax.fori_loop(0, heads, step, 0)
    attend(heads - 1)

    weight_local(heads - 1).wait()
    weight_send(heads - 1).wait_recv()
    for at, count in column_chunks(width):
        mine[:, at:at + count] = jnp.dot(
            att_all[heads - 1, :, att_columns(0, span)], w_last[own_rows, at:at + count],
            preferred_element_type=jnp.float32)

    for which in range(2):
        @pl.when(has_up)
        def _():
            sent(which, zs_sem, {"seq": seq + 2}).wait_send()

        @pl.when(sends_near)
        def _():
            sent(which, ys_sem, {"seq": pair}).wait_send()
    for h in range(heads):
        weight_send(h).wait_send()
    for whose, sem in ((core, es_sem), (other, er_sem)):
        view = early.at[:, half_columns(whose, 0, half)]
        pltpu.make_async_copy(view, view, sem).wait()
    pltpu.make_async_copy(
        att_all.at[:, :, att_columns(0, span)], att_all.at[:, :, att_columns(0, span)], as_sem).wait()
    attended_send(heads - 1).wait_recv()


def finish_kernel(w_last, att_all, early, mine, out_hbm, out_s, sem):
    last = att_all.shape[0] - 1
    span = att_all.shape[2] // 2
    theirs = pl.ds(pl.multiple_of((1 - lax.axis_index("head")) * span, span), span)
    copies = []
    for n, (at, count) in enumerate(column_chunks(mine.shape[1])):
        here = slice(at, at + count)
        out_s[:, here] = (early[:, here].astype(jnp.float32) + (mine[:, here] + jnp.dot(
            att_all[last, :, theirs], w_last[theirs, here],
            preferred_element_type=jnp.float32))).astype(jnp.bfloat16)
        copy = pltpu.make_async_copy(
            out_s.at[:, pl.ds(at, count)], out_hbm.at[:, pl.ds(at, count)], sem.at[n])
        copy.start()
        copies.append(copy)
    for copy in copies:
        copy.wait()


def shards(queries, keys, values, segments, out_weight):
    rows = queries.shape[0]
    assert 2 * rows == ATTENTION_SPAN
    heads = keys.shape[1] // HEAD_SIZE
    query_heads = queries.shape[1] // HEAD_SIZE
    span = query_heads // heads * HEAD_SIZE
    width = out_weight.shape[1]
    seg = segments.reshape(segments.shape[0] // rows, 1, rows)
    dma = pltpu.SemaphoreType.DMA
    anywhere = pl.BlockSpec(memory_space=pltpu.HBM)
    here = pl.BlockSpec(memory_space=pltpu.VMEM)
    bf16, f32 = jnp.bfloat16, jnp.float32
    pieces = heads * 2 * PIECES
    w_last, att_all, early, mine = pl.pallas_call(
        attend_kernel,
        out_shape=(
            pltpu.VMEM((2 * span, width), bf16),
            pltpu.VMEM((heads, rows, 2 * span), bf16),
            pltpu.VMEM((rows, width), bf16),
            pltpu.VMEM((rows, width), f32),
        ),
        in_specs=[anywhere] * 5,
        out_specs=(here,) * 4,
        scratch_shapes=[
            pltpu.VMEM((heads - 1, 2 * span, width // 2), bf16),
            pltpu.VMEM((rows, width // 2), f32),
            pltpu.VMEM(seg.shape, seg.dtype),
            pltpu.VMEM(queries.shape, bf16),
            pltpu.VMEM((3 * rows, keys.shape[1]), bf16),
            pltpu.VMEM((3 * rows, keys.shape[1]), bf16),
            pltpu.VMEM((query_heads, rows, 2 * HEAD_SIZE), f32),
            pltpu.VMEM((query_heads, rows, HEAD_SIZE), f32),
            pltpu.VMEM((query_heads // heads, rows, 2 * rows), bf16),
            pltpu.VMEM((rows, 3 * rows), f32),
            dma((4,)), dma((2,)), dma((pieces,)), dma((2,)), dma((2 * heads,)),
            dma((heads,)), dma((heads,)), dma((heads,)), dma, dma((heads,)), dma, dma,
        ],
        compiler_params=pltpu.CompilerParams(
            collective_id=0, has_side_effects=True, vmem_limit_bytes=34 * 1024 * 1024),
    )(queries, keys, values, pltpu.with_memory_space_constraint(seg, pltpu.HBM), out_weight)
    return pl.pallas_call(
        finish_kernel,
        out_shape=jax.ShapeDtypeStruct((rows, width), bf16),
        in_specs=[here] * 4,
        out_specs=anywhere,
        scratch_shapes=[
            pltpu.VMEM((rows, width), bf16), dma((len(column_chunks(width)),)),
        ],
        compiler_params=pltpu.CompilerParams(vmem_limit_bytes=12 * 1024 * 1024),
    )(w_last, att_all, early, mine)


def solution(mesh):
    placed = (
        P(("groups", "seq"), "head"),
        P(("groups", "seq"), "head"),
        P(("groups", "seq"), "head"),
        P("groups"),
        P("head", None),
    )
    return jax.shard_map(
        shards, mesh=mesh, in_specs=placed, out_specs=P(("groups", "seq"), None), check_vma=False
    )
```

```python
import jax
import jax.numpy as jnp
from jax import lax
from jax.experimental import pallas as pl
from jax.experimental.pallas import tpu as pltpu
from jax.sharding import PartitionSpec as P

HEAD_SIZE = 128
SCALAR = 168
ATTENTION_SPAN = 1024
LOG2E = 1.4426950408889634
QUERY_TILE = 256
PIECES = 2
COLUMN_STEP = 768
MESH = pl.DeviceIdType.MESH
FACTOR = SCALAR ** (-0.5) * LOG2E


def column_chunks(width):
    return [(at, min(COLUMN_STEP, width - at)) for at in range(0, width, COLUMN_STEP)]


def attend_kernel(
    q_hbm, k_hbm, v_hbm, seg_hbm, w_hbm, w_last, att_all, early, mine,
    w_early, acc, seg_ref, q_s, k_s, v_s, part, part_top, probs, bias,
    own_sem, zs_sem, zr_sem, ys_sem, yr_sem, w_sem, ws_sem, wr_sem, as_sem, ar_sem, es_sem, er_sem,
):
    heads = att_all.shape[0]
    rows = q_s.shape[0]
    span = att_all.shape[2] // 2
    group = span // HEAD_SIZE
    width = mine.shape[1]
    half = acc.shape[1]
    tile = QUERY_TILE
    tiles = rows // tile
    size = rows // PIECES
    steps = 2 * PIECES
    seq = lax.axis_index("seq")
    core = lax.axis_index("head")
    peers = lax.axis_size("seq")
    odd = lax.rem(seq, 2)
    pair = seq + 1 - 2 * odd
    other = 1 - core
    chunks = column_chunks(half)
    has_up = seq + 2 < peers
    has_down = seq >= 2
    even = odd == 0
    sends_near = jnp.logical_or(even, seq >= 3)
    relays = jnp.logical_and(odd == 1, seq >= 3)
    takes_far = jnp.logical_and(even, has_down)
    gets_near = seq >= 1

    def head_columns(h):
        return pl.ds(pl.multiple_of(h * HEAD_SIZE, HEAD_SIZE), HEAD_SIZE)

    def piece(j):
        which, part_of = divmod(j, PIECES)
        return ((k_hbm, k_s), (v_hbm, v_s))[which], part_of * size

    def far(h, j):
        (src, dst), at = piece(j)
        return pltpu.make_async_remote_copy(
            src_ref=src.at[pl.ds(at, size), head_columns(h)],
            dst_ref=dst.at[pl.ds(at, size), head_columns(h)],
            send_sem=zs_sem.at[j // PIECES], recv_sem=zr_sem.at[h * steps + j],
            device_id={"seq": seq + 2}, device_id_type=MESH)

    def near(h, j):
        (src, dst), at = piece(j)
        return pltpu.make_async_remote_copy(
            src_ref=src.at[pl.ds(at, size), head_columns(h)],
            dst_ref=dst.at[pl.ds(rows + at, size), head_columns(h)],
            send_sem=ys_sem.at[j // PIECES], recv_sem=yr_sem.at[2 * h + j // PIECES],
            device_id={"seq": pair}, device_id_type=MESH)

    def relay(h, j):
        (_, dst), at = piece(j)
        return pltpu.make_async_remote_copy(
            src_ref=dst.at[pl.ds(at, size), head_columns(h)],
            dst_ref=dst.at[pl.ds(rows + at, size), head_columns(h)],
            send_sem=ys_sem.at[j // PIECES], recv_sem=yr_sem.at[2 * h + j // PIECES],
            device_id={"seq": pair}, device_id_type=MESH)

    def sent(which, sems, device):
        src, dst = ((k_hbm, k_s), (v_hbm, v_s))[which]
        return pltpu.make_async_remote_copy(
            src_ref=src, dst_ref=dst.at[pl.ds(0, rows), :],
            send_sem=sems.at[which], recv_sem=zr_sem.at[0],
            device_id=device, device_id_type=MESH)

    own_copies = [
        pltpu.make_async_copy(q_hbm, q_s, own_sem.at[0]),
        pltpu.make_async_copy(k_hbm, k_s.at[pl.ds(2 * rows, rows), :], own_sem.at[1]),
        pltpu.make_async_copy(v_hbm, v_s.at[pl.ds(2 * rows, rows), :], own_sem.at[2]),
        pltpu.make_async_copy(seg_hbm, seg_ref, own_sem.at[3]),
    ]

    own_rows = pl.ds(pl.multiple_of(core * span, span), span)
    other_rows = pl.ds(pl.multiple_of(other * span, span), span)

    def half_columns(which, at, count):
        return pl.ds(pl.multiple_of(which * half + at, HEAD_SIZE), count)

    def weight_copy(h, whose):
        src = w_hbm.at[pl.ds(h * span, span)]
        if h == heads - 1:
            return src, w_last.at[own_rows]
        return src.at[:, half_columns(whose, 0, half)], w_early.at[h, own_rows]

    def weight_local(h):
        src, dst = weight_copy(h, core)
        return pltpu.make_async_copy(src, dst, w_sem.at[h])

    def weight_send(h):
        src, dst = weight_copy(h, other)
        return pltpu.make_async_remote_copy(
            src_ref=src, dst_ref=dst, send_sem=ws_sem.at[h], recv_sem=wr_sem.at[h],
            device_id={"head": other}, device_id_type=MESH)

    def early_send(at, count):
        view = early.at[:, half_columns(core, at, count)]
        return pltpu.make_async_remote_copy(
            src_ref=view, dst_ref=view, send_sem=es_sem, recv_sem=er_sem,
            device_id={"head": other}, device_id_type=MESH)

    def att_columns(at, count):
        return pl.ds(pl.multiple_of(core * span + at, HEAD_SIZE), count)

    def attended_send(h):
        view = att_all.at[h, :, att_columns(0, span)]
        return pltpu.make_async_remote_copy(
            src_ref=view, dst_ref=view, send_sem=as_sem, recv_sem=ar_sem.at[h],
            device_id={"head": other}, device_id_type=MESH)

    for copy in own_copies:
        copy.start()
    for h in range(heads):
        weight_local(h).start()

    barrier = pltpu.get_barrier_semaphore()
    pl.semaphore_signal(barrier, inc=1, device_id={"head": other}, device_id_type=MESH)
    pl.semaphore_signal(barrier, inc=1, device_id={"seq": pair}, device_id_type=MESH)

    @pl.when(has_up)
    def _():
        pl.semaphore_signal(barrier, inc=1, device_id={"seq": seq + 2}, device_id_type=MESH)

    @pl.when(has_down)
    def _():
        pl.semaphore_signal(barrier, inc=1, device_id={"seq": seq - 2}, device_id_type=MESH)

    pl.semaphore_wait(
        barrier, 2 + jnp.minimum(peers - 1 - seq, 2) // 2 + jnp.minimum(seq, 2) // 2)

    for h in range(heads):
        @pl.when(has_up)
        def _():
            for j in range(steps):
                far(h, j).start()

        @pl.when(even)
        def _():
            for j in range(steps):
                near(h, j).start()

        weight_send(h).start()

    @pl.when(jnp.logical_not(has_down))
    def _():
        k_s[0:rows, :] = jnp.zeros((rows, k_s.shape[1]), k_s.dtype)
        v_s[0:rows, :] = jnp.zeros((rows, v_s.shape[1]), v_s.dtype)

    @pl.when(jnp.logical_not(gets_near))
    def _():
        k_s[rows:2 * rows, :] = jnp.zeros((rows, k_s.shape[1]), k_s.dtype)
        v_s[rows:2 * rows, :] = jnp.zeros((rows, v_s.shape[1]), v_s.dtype)

    own_copies[3].wait()
    span_all = 3 * rows
    seg_own = seg_ref[seq]
    seg_keys = jnp.concatenate([
        seg_ref[jnp.maximum(seq - 2, 0)] - jnp.where(has_down, 0, 1000),
        seg_ref[jnp.maximum(seq - 1, 0)] - jnp.where(gets_near, 0, 1000),
        seg_own,
    ], axis=1).astype(jnp.float32)
    for n in range(rows // 128):
        here = slice(n * 128, (n + 1) * 128)
        seg_query = jnp.broadcast_to(
            seg_own[:, here].astype(jnp.float32), (128, 128)).T[:, :1]
        r = n * 128 + lax.broadcasted_iota(jnp.int32, (128, span_all), 0)
        c = lax.broadcasted_iota(jnp.int32, (128, span_all), 1)
        inside = (c > r) & (c <= r + 2 * rows)
        bias[here, :] = jnp.where(inside & (seg_keys == seg_query), 0.0, -1e30)
    acc[...] = jnp.zeros_like(acc)

    def with_ones(value):
        return jnp.concatenate([value, jnp.ones(value.shape, value.dtype)], axis=1)

    def query_columns(h, g):
        return pl.ds(pl.multiple_of(h * span, HEAD_SIZE) + g * HEAD_SIZE, HEAD_SIZE)

    halo = 2 * rows

    def score(h, g, lines, keys):
        return lax.dot_general(
            q_s[lines, query_columns(h, g)], k_s[keys, head_columns(h)],
            (((1,), (1,)), ((), ())), preferred_element_type=jnp.float32) + bias[lines, keys]

    def own_phase(h, b):
        lines, keys = slice(b * tile, (b + 1) * tile), slice(halo, halo + (b + 1) * tile)
        value = with_ones(v_s[keys, head_columns(h)])
        for g in range(group):
            n = h * group + g
            scores = score(h, g, lines, keys)
            top = jnp.max(scores, axis=1, keepdims=True)
            weights = jnp.exp2((scores - top) * FACTOR).astype(jnp.bfloat16)
            part[n, lines, :] = jnp.dot(weights, value, preferred_element_type=jnp.float32)
            part_top[n, lines, :] = jnp.broadcast_to(top, (tile, HEAD_SIZE))

    def halo_weights(h, b):
        lines, keys = slice(b * tile, (b + 1) * tile), slice(b * tile, halo)
        for g in range(group):
            n = h * group + g
            scores = score(h, g, lines, keys)
            before = part_top[n, lines, :]
            top = jnp.maximum(jnp.max(scores, axis=1, keepdims=True), before[:, :1])
            probs[g, lines, keys] = jnp.exp2((scores - top) * FACTOR).astype(jnp.bfloat16)
            part_top[n, lines, :] = jnp.exp2((before - top) * FACTOR)

    def halo_values(h, b):
        lines, keys = slice(b * tile, (b + 1) * tile), slice(b * tile, halo)
        value = with_ones(v_s[keys, head_columns(h)])
        for g in range(group):
            n = h * group + g
            faded = part_top[n, lines, :]
            mix = part[n, lines, :] * jnp.concatenate([faded, faded], axis=1) + jnp.dot(
                probs[g, lines, keys], value, preferred_element_type=jnp.float32)
            att_all[h, lines, att_columns(g * HEAD_SIZE, HEAD_SIZE)] = (
                mix[:, :HEAD_SIZE] / mix[:, HEAD_SIZE:]).astype(jnp.bfloat16)

    def forward(h, j):
        @pl.when(relays)
        def _():
            far(h, j).wait_recv()
            relay(h, j).start()

    for copy in own_copies[:3]:
        copy.wait()

    def own_step(h, carry):
        for b in range(tiles):
            own_phase(h, b)
        for j, after in ((0, 0), (1, 1), (2, heads - 1)):
            @pl.when(h == after)
            def _():
                forward(0, j)
        return carry

    lax.fori_loop(0, heads, own_step, 0)

    def halo_there(h, which):
        @pl.when(takes_far)
        def _():
            for j in range(which * PIECES, (which + 1) * PIECES):
                far(h, j).wait_recv()

        @pl.when(gets_near)
        def _():
            view = (k_s, v_s)[which].at[pl.ds(rows, rows), head_columns(h)]
            pltpu.make_async_copy(view, view, yr_sem.at[2 * h + which]).wait()

    def attend(h):
        halo_there(h, 1)
        for b in range(tiles):
            halo_values(h, b)
        attended_send(h).start()

    def step(h, carry):
        def product(some):
            for at, count in some:
                acc[:, at:at + count] += jnp.dot(
                    att_all[h - 1, :, pl.ds(pl.multiple_of(other * span, span), span)],
                    w_early[h - 1, other_rows, at:at + count],
                    preferred_element_type=jnp.float32)

            @pl.when(h == heads - 1)
            def _():
                for at, count in some:
                    early[:, half_columns(core, at, count)] = (
                        acc[:, at:at + count].astype(jnp.bfloat16))
                    early_send(at, count).start()

        @pl.when(h >= 1)
        def _():
            forward(h, 0)
            attend(h - 1)
            forward(h, 1)
            view = w_early.at[h - 1, own_rows]
            pltpu.make_async_copy(view, view, w_sem.at[h - 1]).wait()
            for at, count in chunks:
                acc[:, at:at + count] += jnp.dot(
                    att_all[h - 1, :, att_columns(0, span)],
                    w_early[h - 1, own_rows, at:at + count],
                    preferred_element_type=jnp.float32)
            attended_send(h - 1).wait_recv()
            view = w_early.at[h - 1, other_rows]
            pltpu.make_async_copy(view, view, wr_sem.at[h - 1]).wait()
            product(chunks[:2])
            forward(h, 2)
            product(chunks[2:])

        forward(h, 3)
        halo_there(h, 0)
        for b in range(tiles):
            halo_weights(h, b)
        return carry

    lax.fori_loop(0, heads, step, 0)
    attend(heads - 1)

    weight_local(heads - 1).wait()
    weight_send(heads - 1).wait_recv()
    for at, count in column_chunks(width):
        mine[:, at:at + count] = jnp.dot(
            att_all[heads - 1, :, att_columns(0, span)], w_last[own_rows, at:at + count],
            preferred_element_type=jnp.float32)

    for which in range(2):
        @pl.when(has_up)
        def _():
            sent(which, zs_sem, {"seq": seq + 2}).wait_send()

        @pl.when(sends_near)
        def _():
            sent(which, ys_sem, {"seq": pair}).wait_send()
    for h in range(heads):
        weight_send(h).wait_send()
    for whose, sem in ((core, es_sem), (other, er_sem)):
        view = early.at[:, half_columns(whose, 0, half)]
        pltpu.make_async_copy(view, view, sem).wait()
    pltpu.make_async_copy(
        att_all.at[:, :, att_columns(0, span)], att_all.at[:, :, att_columns(0, span)], as_sem).wait()
    attended_send(heads - 1).wait_recv()


def finish_kernel(w_last, att_all, early, mine, out_hbm, out_s, sem):
    last = att_all.shape[0] - 1
    span = att_all.shape[2] // 2
    theirs = pl.ds(pl.multiple_of((1 - lax.axis_index("head")) * span, span), span)
    copies = []
    for n, (at, count) in enumerate(column_chunks(mine.shape[1])):
        here = slice(at, at + count)
        out_s[:, here] = (early[:, here].astype(jnp.float32) + (mine[:, here] + jnp.dot(
            att_all[last, :, theirs], w_last[theirs, here],
            preferred_element_type=jnp.float32))).astype(jnp.bfloat16)
        copy = pltpu.make_async_copy(
            out_s.at[:, pl.ds(at, count)], out_hbm.at[:, pl.ds(at, count)], sem.at[n])
        copy.start()
        copies.append(copy)
    for copy in copies:
        copy.wait()


def shards(queries, keys, values, segments, out_weight):
    rows = queries.shape[0]
    assert 2 * rows == ATTENTION_SPAN
    heads = keys.shape[1] // HEAD_SIZE
    query_heads = queries.shape[1] // HEAD_SIZE
    span = query_heads // heads * HEAD_SIZE
    width = out_weight.shape[1]
    seg = segments.reshape(segments.shape[0] // rows, 1, rows)
    dma = pltpu.SemaphoreType.DMA
    anywhere = pl.BlockSpec(memory_space=pltpu.HBM)
    here = pl.BlockSpec(memory_space=pltpu.VMEM)
    bf16, f32 = jnp.bfloat16, jnp.float32
    pieces = heads * 2 * PIECES
    w_last, att_all, early, mine = pl.pallas_call(
        attend_kernel,
        out_shape=(
            pltpu.VMEM((2 * span, width), bf16),
            pltpu.VMEM((heads, rows, 2 * span), bf16),
            pltpu.VMEM((rows, width), bf16),
            pltpu.VMEM((rows, width), f32),
        ),
        in_specs=[anywhere] * 5,
        out_specs=(here,) * 4,
        scratch_shapes=[
            pltpu.VMEM((heads - 1, 2 * span, width // 2), bf16),
            pltpu.VMEM((rows, width // 2), f32),
            pltpu.VMEM(seg.shape, seg.dtype),
            pltpu.VMEM(queries.shape, bf16),
            pltpu.VMEM((3 * rows, keys.shape[1]), bf16),
            pltpu.VMEM((3 * rows, keys.shape[1]), bf16),
            pltpu.VMEM((query_heads, rows, 2 * HEAD_SIZE), f32),
            pltpu.VMEM((query_heads, rows, HEAD_SIZE), f32),
            pltpu.VMEM((query_heads // heads, rows, 2 * rows), bf16),
            pltpu.VMEM((rows, 3 * rows), f32),
            dma((4,)), dma((2,)), dma((pieces,)), dma((2,)), dma((2 * heads,)),
            dma((heads,)), dma((heads,)), dma((heads,)), dma, dma((heads,)), dma, dma,
        ],
        compiler_params=pltpu.CompilerParams(
            collective_id=0, has_side_effects=True, vmem_limit_bytes=34 * 1024 * 1024),
    )(queries, keys, values, pltpu.with_memory_space_constraint(seg, pltpu.HBM), out_weight)
    return pl.pallas_call(
        finish_kernel,
        out_shape=jax.ShapeDtypeStruct((rows, width), bf16),
        in_specs=[here] * 4,
        out_specs=anywhere,
        scratch_shapes=[
            pltpu.VMEM((rows, width), bf16), dma((len(column_chunks(width)),)),
        ],
        compiler_params=pltpu.CompilerParams(vmem_limit_bytes=12 * 1024 * 1024),
    )(w_last, att_all, early, mine)


def solution(mesh):
    placed = (
        P(("groups", "seq"), "head"),
        P(("groups", "seq"), "head"),
        P(("groups", "seq"), "head"),
        P("groups"),
        P("head", None),
    )
    return jax.shard_map(
        shards, mesh=mesh, in_specs=placed, out_specs=P(("groups", "seq"), None), check_vma=False
    )
```

```python
import jax
import jax.numpy as jnp
from jax import lax
from jax.experimental import pallas as pl
from jax.experimental.pallas import tpu as pltpu
from jax.sharding import PartitionSpec as P

HEAD_SIZE = 128
SCALAR = 168
ATTENTION_SPAN = 1024
LOG2E = 1.4426950408889634
QUERY_TILE = 256
PIECES = 2
COLUMN_STEP = 768
MESH = pl.DeviceIdType.MESH
FACTOR = SCALAR ** (-0.5) * LOG2E


def column_chunks(width):
    return [(at, min(COLUMN_STEP, width - at)) for at in range(0, width, COLUMN_STEP)]


def attend_kernel(
    q_hbm, k_hbm, v_hbm, seg_hbm, w_hbm, w_last, att_all, early, mine,
    w_early, acc, seg_ref, q_s, k_s, v_s, part, part_top, probs, bias,
    own_sem, zs_sem, zr_sem, ys_sem, yr_sem, w_sem, ws_sem, wr_sem, as_sem, ar_sem, es_sem, er_sem,
):
    heads = att_all.shape[0]
    rows = q_s.shape[0]
    span = att_all.shape[2] // 2
    group = span // HEAD_SIZE
    width = mine.shape[1]
    half = acc.shape[1]
    tile = QUERY_TILE
    tiles = rows // tile
    size = rows // PIECES
    steps = 2 * PIECES
    seq = lax.axis_index("seq")
    core = lax.axis_index("head")
    peers = lax.axis_size("seq")
    odd = lax.rem(seq, 2)
    pair = seq + 1 - 2 * odd
    other = 1 - core
    chunks = column_chunks(half)
    has_up = seq + 2 < peers
    has_down = seq >= 2
    even = odd == 0
    sends_near = jnp.logical_or(even, seq >= 3)
    relays = jnp.logical_and(odd == 1, seq >= 3)
    takes_far = jnp.logical_and(even, has_down)
    gets_near = seq >= 1

    def head_columns(h):
        return pl.ds(pl.multiple_of(h * HEAD_SIZE, HEAD_SIZE), HEAD_SIZE)

    def piece(j):
        which, part_of = divmod(j, PIECES)
        return ((k_hbm, k_s), (v_hbm, v_s))[which], part_of * size

    def far(h, j):
        (src, dst), at = piece(j)
        return pltpu.make_async_remote_copy(
            src_ref=src.at[pl.ds(at, size), head_columns(h)],
            dst_ref=dst.at[pl.ds(at, size), head_columns(h)],
            send_sem=zs_sem.at[j // PIECES], recv_sem=zr_sem.at[h * steps + j],
            device_id={"seq": seq + 2}, device_id_type=MESH)

    def near(h, j):
        (src, dst), at = piece(j)
        return pltpu.make_async_remote_copy(
            src_ref=src.at[pl.ds(at, size), head_columns(h)],
            dst_ref=dst.at[pl.ds(rows + at, size), head_columns(h)],
            send_sem=ys_sem.at[j // PIECES], recv_sem=yr_sem.at[2 * h + j // PIECES],
            device_id={"seq": pair}, device_id_type=MESH)

    def relay(h, j):
        (_, dst), at = piece(j)
        return pltpu.make_async_remote_copy(
            src_ref=dst.at[pl.ds(at, size), head_columns(h)],
            dst_ref=dst.at[pl.ds(rows + at, size), head_columns(h)],
            send_sem=ys_sem.at[j // PIECES], recv_sem=yr_sem.at[2 * h + j // PIECES],
            device_id={"seq": pair}, device_id_type=MESH)

    def sent(which, sems, device):
        src, dst = ((k_hbm, k_s), (v_hbm, v_s))[which]
        return pltpu.make_async_remote_copy(
            src_ref=src, dst_ref=dst.at[pl.ds(0, rows), :],
            send_sem=sems.at[which], recv_sem=zr_sem.at[0],
            device_id=device, device_id_type=MESH)

    own_copies = [
        pltpu.make_async_copy(q_hbm, q_s, own_sem.at[0]),
        pltpu.make_async_copy(k_hbm, k_s.at[pl.ds(2 * rows, rows), :], own_sem.at[1]),
        pltpu.make_async_copy(v_hbm, v_s.at[pl.ds(2 * rows, rows), :], own_sem.at[2]),
        pltpu.make_async_copy(seg_hbm, seg_ref, own_sem.at[3]),
    ]

    own_rows = pl.ds(pl.multiple_of(core * span, span), span)
    other_rows = pl.ds(pl.multiple_of(other * span, span), span)

    def half_columns(which, at, count):
        return pl.ds(pl.multiple_of(which * half + at, HEAD_SIZE), count)

    def weight_copy(h, whose):
        src = w_hbm.at[pl.ds(h * span, span)]
        if h == heads - 1:
            return src, w_last.at[own_rows]
        return src.at[:, half_columns(whose, 0, half)], w_early.at[h, own_rows]

    def weight_local(h):
        src, dst = weight_copy(h, core)
        return pltpu.make_async_copy(src, dst, w_sem.at[h])

    def weight_send(h):
        src, dst = weight_copy(h, other)
        return pltpu.make_async_remote_copy(
            src_ref=src, dst_ref=dst, send_sem=ws_sem.at[h], recv_sem=wr_sem.at[h],
            device_id={"head": other}, device_id_type=MESH)

    def early_send(at, count):
        view = early.at[:, half_columns(core, at, count)]
        return pltpu.make_async_remote_copy(
            src_ref=view, dst_ref=view, send_sem=es_sem, recv_sem=er_sem,
            device_id={"head": other}, device_id_type=MESH)

    def att_columns(at, count):
        return pl.ds(pl.multiple_of(core * span + at, HEAD_SIZE), count)

    def attended_send(h):
        view = att_all.at[h, :, att_columns(0, span)]
        return pltpu.make_async_remote_copy(
            src_ref=view, dst_ref=view, send_sem=as_sem, recv_sem=ar_sem.at[h],
            device_id={"head": other}, device_id_type=MESH)

    for copy in own_copies:
        copy.start()
    for h in range(heads):
        weight_local(h).start()

    barrier = pltpu.get_barrier_semaphore()
    pl.semaphore_signal(barrier, inc=1, device_id={"head": other}, device_id_type=MESH)
    pl.semaphore_signal(barrier, inc=1, device_id={"seq": pair}, device_id_type=MESH)

    @pl.when(has_up)
    def _():
        pl.semaphore_signal(barrier, inc=1, device_id={"seq": seq + 2}, device_id_type=MESH)

    @pl.when(has_down)
    def _():
        pl.semaphore_signal(barrier, inc=1, device_id={"seq": seq - 2}, device_id_type=MESH)

    pl.semaphore_wait(
        barrier, 2 + jnp.minimum(peers - 1 - seq, 2) // 2 + jnp.minimum(seq, 2) // 2)

    for h in range(heads):
        @pl.when(has_up)
        def _():
            for j in range(steps):
                far(h, j).start()

        @pl.when(even)
        def _():
            for j in range(steps):
                near(h, j).start()

        weight_send(h).start()

    @pl.when(jnp.logical_not(has_down))
    def _():
        k_s[0:rows, :] = jnp.zeros((rows, k_s.shape[1]), k_s.dtype)
        v_s[0:rows, :] = jnp.zeros((rows, v_s.shape[1]), v_s.dtype)

    @pl.when(jnp.logical_not(gets_near))
    def _():
        k_s[rows:2 * rows, :] = jnp.zeros((rows, k_s.shape[1]), k_s.dtype)
        v_s[rows:2 * rows, :] = jnp.zeros((rows, v_s.shape[1]), v_s.dtype)

    own_copies[3].wait()
    span_all = 3 * rows
    seg_own = seg_ref[seq]
    seg_keys = jnp.concatenate([
        seg_ref[jnp.maximum(seq - 2, 0)] - jnp.where(has_down, 0, 1000),
        seg_ref[jnp.maximum(seq - 1, 0)] - jnp.where(gets_near, 0, 1000),
        seg_own,
    ], axis=1).astype(jnp.float32)
    for n in range(rows // 128):
        here = slice(n * 128, (n + 1) * 128)
        seg_query = jnp.broadcast_to(
            seg_own[:, here].astype(jnp.float32), (128, 128)).T[:, :1]
        r = n * 128 + lax.broadcasted_iota(jnp.int32, (128, span_all), 0)
        c = lax.broadcasted_iota(jnp.int32, (128, span_all), 1)
        inside = (c > r) & (c <= r + 2 * rows)
        bias[here, :] = jnp.where(inside & (seg_keys == seg_query), 0.0, -1e30)
    acc[...] = jnp.zeros_like(acc)

    def with_ones(value):
        return jnp.concatenate([value, jnp.ones(value.shape, value.dtype)], axis=1)

    def query_columns(h, g):
        return pl.ds(pl.multiple_of(h * span, HEAD_SIZE) + g * HEAD_SIZE, HEAD_SIZE)

    halo = 2 * rows

    def score(h, g, lines, keys):
        return lax.dot_general(
            q_s[lines, query_columns(h, g)], k_s[keys, head_columns(h)],
            (((1,), (1,)), ((), ())), preferred_element_type=jnp.float32) + bias[lines, keys]

    def own_phase(h, b):
        lines, keys = slice(b * tile, (b + 1) * tile), slice(halo, halo + (b + 1) * tile)
        value = with_ones(v_s[keys, head_columns(h)])
        for g in range(group):
            n = h * group + g
            scores = score(h, g, lines, keys)
            top = jnp.max(scores, axis=1, keepdims=True)
            weights = jnp.exp2((scores - top) * FACTOR).astype(jnp.bfloat16)
            part[n, lines, :] = jnp.dot(weights, value, preferred_element_type=jnp.float32)
            part_top[n, lines, :] = jnp.broadcast_to(top, (tile, HEAD_SIZE))

    def halo_weights(h, b):
        lines, keys = slice(b * tile, (b + 1) * tile), slice(b * tile, halo)
        for g in range(group):
            n = h * group + g
            scores = score(h, g, lines, keys)
            before = part_top[n, lines, :]
            top = jnp.maximum(jnp.max(scores, axis=1, keepdims=True), before[:, :1])
            probs[g, lines, keys] = jnp.exp2((scores - top) * FACTOR).astype(jnp.bfloat16)
            part_top[n, lines, :] = jnp.exp2((before - top) * FACTOR)

    def far_values(h, b):
        lines, keys = slice(b * tile, (b + 1) * tile), slice(b * tile, rows)
        value = with_ones(v_s[keys, head_columns(h)])
        for g in range(group):
            n = h * group + g
            faded = part_top[n, lines, :]
            part[n, lines, :] = part[n, lines, :] * jnp.concatenate(
                [faded, faded], axis=1) + jnp.dot(
                    probs[g, lines, keys], value, preferred_element_type=jnp.float32)

    def near_values(h, b):
        lines, keys = slice(b * tile, (b + 1) * tile), slice(rows, halo)
        value = with_ones(v_s[keys, head_columns(h)])
        for g in range(group):
            n = h * group + g
            mix = part[n, lines, :] + jnp.dot(
                probs[g, lines, keys], value, preferred_element_type=jnp.float32)
            att_all[h, lines, att_columns(g * HEAD_SIZE, HEAD_SIZE)] = (
                mix[:, :HEAD_SIZE] / mix[:, HEAD_SIZE:]).astype(jnp.bfloat16)

    def forward(h, j):
        @pl.when(relays)
        def _():
            far(h, j).wait_recv()
            relay(h, j).start()

    for copy in own_copies[:3]:
        copy.wait()

    def own_step(h, carry):
        for b in range(tiles):
            own_phase(h, b)
        for j, after in ((0, 0), (1, 1), (2, heads - 1)):
            @pl.when(h == after)
            def _():
                forward(0, j)
        return carry

    lax.fori_loop(0, heads, own_step, 0)

    def far_there(h, which):
        @pl.when(takes_far)
        def _():
            for j in range(which * PIECES, (which + 1) * PIECES):
                far(h, j).wait_recv()

    def near_there(h, which):
        @pl.when(gets_near)
        def _():
            view = (k_s, v_s)[which].at[pl.ds(rows, rows), head_columns(h)]
            pltpu.make_async_copy(view, view, yr_sem.at[2 * h + which]).wait()

    def attend(h, between=lambda: None):
        far_there(h, 1)
        for b in range(tiles):
            far_values(h, b)
        between()
        near_there(h, 1)
        for b in range(tiles):
            near_values(h, b)
        attended_send(h).start()

    def step(h, carry):
        def product(some):
            def terms(at, count):
                return acc[:, at:at + count] + jnp.dot(
                    att_all[h - 1, :, pl.ds(pl.multiple_of(other * span, span), span)],
                    w_early[h - 1, other_rows, at:at + count],
                    preferred_element_type=jnp.float32)

            @pl.when(h < heads - 1)
            def _():
                for at, count in some:
                    acc[:, at:at + count] = terms(at, count)

            @pl.when(h == heads - 1)
            def _():
                for at, count in some:
                    early[:, half_columns(core, at, count)] = terms(at, count).astype(jnp.bfloat16)
                    early_send(at, count).start()

        @pl.when(h >= 1)
        def _():
            attend(h - 1, lambda: forward(h, 0))
            forward(h, 1)
            view = w_early.at[h - 1, own_rows]
            pltpu.make_async_copy(view, view, w_sem.at[h - 1]).wait()
            for at, count in chunks:
                acc[:, at:at + count] += jnp.dot(
                    att_all[h - 1, :, att_columns(0, span)],
                    w_early[h - 1, own_rows, at:at + count],
                    preferred_element_type=jnp.float32)
            forward(h, 2)
            attended_send(h - 1).wait_recv()
            view = w_early.at[h - 1, other_rows]
            pltpu.make_async_copy(view, view, wr_sem.at[h - 1]).wait()
            product(chunks)

        forward(h, 3)
        far_there(h, 0)
        near_there(h, 0)
        for b in range(tiles):
            halo_weights(h, b)
        return carry

    lax.fori_loop(0, heads, step, 0)
    attend(heads - 1)

    weight_local(heads - 1).wait()
    weight_send(heads - 1).wait_recv()
    for at, count in column_chunks(width):
        mine[:, at:at + count] = jnp.dot(
            att_all[heads - 1, :, att_columns(0, span)], w_last[own_rows, at:at + count],
            preferred_element_type=jnp.float32)

    for which in range(2):
        @pl.when(has_up)
        def _():
            sent(which, zs_sem, {"seq": seq + 2}).wait_send()

        @pl.when(sends_near)
        def _():
            sent(which, ys_sem, {"seq": pair}).wait_send()
    for h in range(heads):
        weight_send(h).wait_send()
    for whose, sem in ((core, es_sem), (other, er_sem)):
        view = early.at[:, half_columns(whose, 0, half)]
        pltpu.make_async_copy(view, view, sem).wait()
    pltpu.make_async_copy(
        att_all.at[:, :, att_columns(0, span)], att_all.at[:, :, att_columns(0, span)], as_sem).wait()
    attended_send(heads - 1).wait_recv()


def finish_kernel(w_last, att_all, early, mine, out_hbm, out_s, sem):
    last = att_all.shape[0] - 1
    span = att_all.shape[2] // 2
    theirs = pl.ds(pl.multiple_of((1 - lax.axis_index("head")) * span, span), span)
    copies = []
    for n, (at, count) in enumerate(column_chunks(mine.shape[1])):
        here = slice(at, at + count)
        out_s[:, here] = (early[:, here].astype(jnp.float32) + (mine[:, here] + jnp.dot(
            att_all[last, :, theirs], w_last[theirs, here],
            preferred_element_type=jnp.float32))).astype(jnp.bfloat16)
        copy = pltpu.make_async_copy(
            out_s.at[:, pl.ds(at, count)], out_hbm.at[:, pl.ds(at, count)], sem.at[n])
        copy.start()
        copies.append(copy)
    for copy in copies:
        copy.wait()


def shards(queries, keys, values, segments, out_weight):
    rows = queries.shape[0]
    assert 2 * rows == ATTENTION_SPAN
    heads = keys.shape[1] // HEAD_SIZE
    query_heads = queries.shape[1] // HEAD_SIZE
    span = query_heads // heads * HEAD_SIZE
    width = out_weight.shape[1]
    seg = segments.reshape(segments.shape[0] // rows, 1, rows)
    dma = pltpu.SemaphoreType.DMA
    anywhere = pl.BlockSpec(memory_space=pltpu.HBM)
    here = pl.BlockSpec(memory_space=pltpu.VMEM)
    bf16, f32 = jnp.bfloat16, jnp.float32
    pieces = heads * 2 * PIECES
    w_last, att_all, early, mine = pl.pallas_call(
        attend_kernel,
        out_shape=(
            pltpu.VMEM((2 * span, width), bf16),
            pltpu.VMEM((heads, rows, 2 * span), bf16),
            pltpu.VMEM((rows, width), bf16),
            pltpu.VMEM((rows, width), f32),
        ),
        in_specs=[anywhere] * 5,
        out_specs=(here,) * 4,
        scratch_shapes=[
            pltpu.VMEM((heads - 1, 2 * span, width // 2), bf16),
            pltpu.VMEM((rows, width // 2), f32),
            pltpu.VMEM(seg.shape, seg.dtype),
            pltpu.VMEM(queries.shape, bf16),
            pltpu.VMEM((3 * rows, keys.shape[1]), bf16),
            pltpu.VMEM((3 * rows, keys.shape[1]), bf16),
            pltpu.VMEM((query_heads, rows, 2 * HEAD_SIZE), f32),
            pltpu.VMEM((query_heads, rows, HEAD_SIZE), f32),
            pltpu.VMEM((query_heads // heads, rows, 2 * rows), bf16),
            pltpu.VMEM((rows, 3 * rows), f32),
            dma((4,)), dma((2,)), dma((pieces,)), dma((2,)), dma((2 * heads,)),
            dma((heads,)), dma((heads,)), dma((heads,)), dma, dma((heads,)), dma, dma,
        ],
        compiler_params=pltpu.CompilerParams(
            collective_id=0, has_side_effects=True, vmem_limit_bytes=34 * 1024 * 1024),
    )(queries, keys, values, pltpu.with_memory_space_constraint(seg, pltpu.HBM), out_weight)
    return pl.pallas_call(
        finish_kernel,
        out_shape=jax.ShapeDtypeStruct((rows, width), bf16),
        in_specs=[here] * 4,
        out_specs=anywhere,
        scratch_shapes=[
            pltpu.VMEM((rows, width), bf16), dma((len(column_chunks(width)),)),
        ],
        compiler_params=pltpu.CompilerParams(vmem_limit_bytes=12 * 1024 * 1024),
    )(w_last, att_all, early, mine)


def solution(mesh):
    placed = (
        P(("groups", "seq"), "head"),
        P(("groups", "seq"), "head"),
        P(("groups", "seq"), "head"),
        P("groups"),
        P("head", None),
    )
    return jax.shard_map(
        shards, mesh=mesh, in_specs=placed, out_specs=P(("groups", "seq"), None), check_vma=False
    )
```

```python
import jax
import jax.numpy as jnp
from jax import lax
from jax.experimental import pallas as pl
from jax.experimental.pallas import tpu as pltpu
from jax.sharding import PartitionSpec as P

HEAD_SIZE = 128
SCALAR = 168
ATTENTION_SPAN = 1024
LOG2E = 1.4426950408889634
QUERY_TILE = 256
PIECES = 2
COLUMN_STEP = 768
MESH = pl.DeviceIdType.MESH
FACTOR = SCALAR ** (-0.5) * LOG2E


def column_chunks(width):
    return [(at, min(COLUMN_STEP, width - at)) for at in range(0, width, COLUMN_STEP)]


def attend_kernel(
    q_hbm, k_hbm, v_hbm, seg_hbm, w_hbm, w_last, att_all, early, mine,
    w_early, acc, seg_ref, q_s, k_s, v_s, part, part_top, probs, bias,
    own_sem, zs_sem, zr_sem, ys_sem, yr_sem, w_sem, ws_sem, wr_sem, as_sem, ar_sem, es_sem, er_sem,
):
    heads = att_all.shape[0]
    rows = q_s.shape[0]
    span = att_all.shape[2] // 2
    group = span // HEAD_SIZE
    width = mine.shape[1]
    half = acc.shape[1]
    tile = QUERY_TILE
    tiles = rows // tile
    size = rows // PIECES
    steps = 2 * PIECES
    seq = lax.axis_index("seq")
    core = lax.axis_index("head")
    peers = lax.axis_size("seq")
    odd = lax.rem(seq, 2)
    pair = seq + 1 - 2 * odd
    other = 1 - core
    chunks = column_chunks(half)
    has_up = seq + 2 < peers
    has_down = seq >= 2
    even = odd == 0
    sends_near = jnp.logical_or(even, seq >= 3)
    relays = jnp.logical_and(odd == 1, seq >= 3)
    takes_far = jnp.logical_and(even, has_down)
    gets_near = seq >= 1

    def head_columns(h):
        return pl.ds(pl.multiple_of(h * HEAD_SIZE, HEAD_SIZE), HEAD_SIZE)

    def piece(j):
        which, part_of = divmod(j, PIECES)
        return ((k_hbm, k_s), (v_hbm, v_s))[which], part_of * size

    def far(h, j):
        (src, dst), at = piece(j)
        return pltpu.make_async_remote_copy(
            src_ref=src.at[pl.ds(at, size), head_columns(h)],
            dst_ref=dst.at[pl.ds(at, size), head_columns(h)],
            send_sem=zs_sem.at[j // PIECES], recv_sem=zr_sem.at[h * steps + j],
            device_id={"seq": seq + 2}, device_id_type=MESH)

    def near(h, j):
        (src, dst), at = piece(j)
        return pltpu.make_async_remote_copy(
            src_ref=src.at[pl.ds(at, size), head_columns(h)],
            dst_ref=dst.at[pl.ds(rows + at, size), head_columns(h)],
            send_sem=ys_sem.at[j // PIECES], recv_sem=yr_sem.at[2 * h + j // PIECES],
            device_id={"seq": pair}, device_id_type=MESH)

    def relay(h, j):
        (_, dst), at = piece(j)
        return pltpu.make_async_remote_copy(
            src_ref=dst.at[pl.ds(at, size), head_columns(h)],
            dst_ref=dst.at[pl.ds(rows + at, size), head_columns(h)],
            send_sem=ys_sem.at[j // PIECES], recv_sem=yr_sem.at[2 * h + j // PIECES],
            device_id={"seq": pair}, device_id_type=MESH)

    def sent(which, sems, device):
        src, dst = ((k_hbm, k_s), (v_hbm, v_s))[which]
        return pltpu.make_async_remote_copy(
            src_ref=src, dst_ref=dst.at[pl.ds(0, rows), :],
            send_sem=sems.at[which], recv_sem=zr_sem.at[0],
            device_id=device, device_id_type=MESH)

    own_copies = [
        pltpu.make_async_copy(q_hbm, q_s, own_sem.at[0]),
        pltpu.make_async_copy(k_hbm, k_s.at[pl.ds(2 * rows, rows), :], own_sem.at[1]),
        pltpu.make_async_copy(v_hbm, v_s.at[pl.ds(2 * rows, rows), :], own_sem.at[2]),
        pltpu.make_async_copy(seg_hbm, seg_ref, own_sem.at[3]),
    ]

    own_rows = pl.ds(pl.multiple_of(core * span, span), span)
    other_rows = pl.ds(pl.multiple_of(other * span, span), span)

    def half_columns(which, at, count):
        return pl.ds(pl.multiple_of(which * half + at, HEAD_SIZE), count)

    def weight_copy(h, whose):
        src = w_hbm.at[pl.ds(h * span, span)]
        if h == heads - 1:
            return src, w_last.at[own_rows]
        return src.at[:, half_columns(whose, 0, half)], w_early.at[h, own_rows]

    def weight_local(h):
        src, dst = weight_copy(h, core)
        return pltpu.make_async_copy(src, dst, w_sem.at[h])

    def weight_send(h):
        src, dst = weight_copy(h, other)
        return pltpu.make_async_remote_copy(
            src_ref=src, dst_ref=dst, send_sem=ws_sem.at[h], recv_sem=wr_sem.at[h],
            device_id={"head": other}, device_id_type=MESH)

    def early_send(at, count):
        view = early.at[:, half_columns(core, at, count)]
        return pltpu.make_async_remote_copy(
            src_ref=view, dst_ref=view, send_sem=es_sem, recv_sem=er_sem,
            device_id={"head": other}, device_id_type=MESH)

    def att_columns(at, count):
        return pl.ds(pl.multiple_of(core * span + at, HEAD_SIZE), count)

    def attended_send(h):
        view = att_all.at[h, :, att_columns(0, span)]
        return pltpu.make_async_remote_copy(
            src_ref=view, dst_ref=view, send_sem=as_sem, recv_sem=ar_sem.at[h],
            device_id={"head": other}, device_id_type=MESH)

    for copy in own_copies:
        copy.start()
    for h in range(heads):
        weight_local(h).start()

    barrier = pltpu.get_barrier_semaphore()
    pl.semaphore_signal(barrier, inc=1, device_id={"head": other}, device_id_type=MESH)
    pl.semaphore_signal(barrier, inc=1, device_id={"seq": pair}, device_id_type=MESH)

    @pl.when(has_up)
    def _():
        pl.semaphore_signal(barrier, inc=1, device_id={"seq": seq + 2}, device_id_type=MESH)

    @pl.when(has_down)
    def _():
        pl.semaphore_signal(barrier, inc=1, device_id={"seq": seq - 2}, device_id_type=MESH)

    pl.semaphore_wait(
        barrier, 2 + jnp.minimum(peers - 1 - seq, 2) // 2 + jnp.minimum(seq, 2) // 2)

    for h in range(heads):
        @pl.when(has_up)
        def _():
            for j in range(steps):
                far(h, j).start()

        @pl.when(even)
        def _():
            for j in range(steps):
                near(h, j).start()

        weight_send(h).start()

    @pl.when(jnp.logical_not(has_down))
    def _():
        k_s[0:rows, :] = jnp.zeros((rows, k_s.shape[1]), k_s.dtype)
        v_s[0:rows, :] = jnp.zeros((rows, v_s.shape[1]), v_s.dtype)

    @pl.when(jnp.logical_not(gets_near))
    def _():
        k_s[rows:2 * rows, :] = jnp.zeros((rows, k_s.shape[1]), k_s.dtype)
        v_s[rows:2 * rows, :] = jnp.zeros((rows, v_s.shape[1]), v_s.dtype)

    own_copies[3].wait()
    span_all = 3 * rows
    seg_own = seg_ref[seq]
    seg_keys = jnp.concatenate([
        seg_ref[jnp.maximum(seq - 2, 0)] - jnp.where(has_down, 0, 1000),
        seg_ref[jnp.maximum(seq - 1, 0)] - jnp.where(gets_near, 0, 1000),
        seg_own,
    ], axis=1).astype(jnp.float32)
    for n in range(rows // 128):
        here = slice(n * 128, (n + 1) * 128)
        seg_query = jnp.broadcast_to(
            seg_own[:, here].astype(jnp.float32), (128, 128)).T[:, :1]
        r = n * 128 + lax.broadcasted_iota(jnp.int32, (128, span_all), 0)
        c = lax.broadcasted_iota(jnp.int32, (128, span_all), 1)
        inside = (c > r) & (c <= r + 2 * rows)
        bias[here, :] = jnp.where(inside & (seg_keys == seg_query), 0.0, -1e30)
    acc[...] = jnp.zeros_like(acc)

    def with_ones(value):
        return jnp.concatenate([value, jnp.ones(value.shape, value.dtype)], axis=1)

    def query_columns(h, g):
        return pl.ds(pl.multiple_of(h * span, HEAD_SIZE) + g * HEAD_SIZE, HEAD_SIZE)

    halo = 2 * rows

    def score(h, g, lines, keys):
        return lax.dot_general(
            q_s[lines, query_columns(h, g)], k_s[keys, head_columns(h)],
            (((1,), (1,)), ((), ())), preferred_element_type=jnp.float32) + bias[lines, keys]

    def own_phase(h, b):
        lines, keys = slice(b * tile, (b + 1) * tile), slice(halo, halo + (b + 1) * tile)
        value = with_ones(v_s[keys, head_columns(h)])
        for g in range(group):
            n = h * group + g
            scores = score(h, g, lines, keys)
            top = jnp.max(scores, axis=1, keepdims=True)
            weights = jnp.exp2((scores - top) * FACTOR).astype(jnp.bfloat16)
            part[n, lines, :] = jnp.dot(weights, value, preferred_element_type=jnp.float32)
            part_top[n, lines, :] = jnp.broadcast_to(top, (tile, HEAD_SIZE))

    def halo_weights(h, b):
        lines, keys = slice(b * tile, (b + 1) * tile), slice(b * tile, halo)
        for g in range(group):
            n = h * group + g
            scores = score(h, g, lines, keys)
            before = part_top[n, lines, :]
            top = jnp.maximum(jnp.max(scores, axis=1, keepdims=True), before[:, :1])
            probs[g, lines, keys] = jnp.exp2((scores - top) * FACTOR).astype(jnp.bfloat16)
            part_top[n, lines, :] = jnp.exp2((before - top) * FACTOR)

    def far_values(h, b):
        lines, keys = slice(b * tile, (b + 1) * tile), slice(b * tile, rows)
        value = with_ones(v_s[keys, head_columns(h)])
        for g in range(group):
            n = h * group + g
            faded = part_top[n, lines, :]
            part[n, lines, :] = part[n, lines, :] * jnp.concatenate(
                [faded, faded], axis=1) + jnp.dot(
                    probs[g, lines, keys], value, preferred_element_type=jnp.float32)

    def near_values(h):
        lines, keys = slice(0, rows), slice(rows, halo)
        value = with_ones(v_s[keys, head_columns(h)])
        for g in range(group):
            n = h * group + g
            mix = part[n, lines, :] + jnp.dot(
                probs[g, lines, keys], value, preferred_element_type=jnp.float32)
            att_all[h, lines, att_columns(g * HEAD_SIZE, HEAD_SIZE)] = (
                mix[:, :HEAD_SIZE] / mix[:, HEAD_SIZE:]).astype(jnp.bfloat16)

    def forward(h, j):
        @pl.when(relays)
        def _():
            far(h, j).wait_recv()
            relay(h, j).start()

    for copy in own_copies[:3]:
        copy.wait()

    def own_step(h, carry):
        for b in range(tiles):
            own_phase(h, b)
        for j, after in ((0, 0), (1, 1), (2, heads - 1)):
            @pl.when(h == after)
            def _():
                forward(0, j)
        return carry

    lax.fori_loop(0, heads, own_step, 0)

    def far_there(h, which):
        @pl.when(takes_far)
        def _():
            for j in range(which * PIECES, (which + 1) * PIECES):
                far(h, j).wait_recv()

    def near_there(h, which):
        @pl.when(gets_near)
        def _():
            view = (k_s, v_s)[which].at[pl.ds(rows, rows), head_columns(h)]
            pltpu.make_async_copy(view, view, yr_sem.at[2 * h + which]).wait()

    def attend(h, between=lambda: None):
        far_there(h, 1)
        for b in range(tiles):
            far_values(h, b)
        between()
        near_there(h, 1)
        near_values(h)
        attended_send(h).start()

    def step(h, carry):
        def product(some):
            def terms(at, count):
                return acc[:, at:at + count] + jnp.dot(
                    att_all[h - 1, :, pl.ds(pl.multiple_of(other * span, span), span)],
                    w_early[h - 1, other_rows, at:at + count],
                    preferred_element_type=jnp.float32)

            @pl.when(h < heads - 1)
            def _():
                for at, count in some:
                    acc[:, at:at + count] = terms(at, count)

            @pl.when(h == heads - 1)
            def _():
                for at, count in some:
                    early[:, half_columns(core, at, count)] = terms(at, count).astype(jnp.bfloat16)
                    early_send(at, count).start()

        @pl.when(h >= 1)
        def _():
            attend(h - 1, lambda: forward(h, 0))
            forward(h, 1)
            view = w_early.at[h - 1, own_rows]
            pltpu.make_async_copy(view, view, w_sem.at[h - 1]).wait()
            for at, count in chunks:
                acc[:, at:at + count] += jnp.dot(
                    att_all[h - 1, :, att_columns(0, span)],
                    w_early[h - 1, own_rows, at:at + count],
                    preferred_element_type=jnp.float32)
            forward(h, 2)
            attended_send(h - 1).wait_recv()
            view = w_early.at[h - 1, other_rows]
            pltpu.make_async_copy(view, view, wr_sem.at[h - 1]).wait()
            product(chunks)

        forward(h, 3)
        far_there(h, 0)
        near_there(h, 0)
        for b in range(tiles):
            halo_weights(h, b)
        return carry

    lax.fori_loop(0, heads, step, 0)
    attend(heads - 1)

    weight_local(heads - 1).wait()
    weight_send(heads - 1).wait_recv()
    for at, count in column_chunks(width):
        mine[:, at:at + count] = jnp.dot(
            att_all[heads - 1, :, att_columns(0, span)], w_last[own_rows, at:at + count],
            preferred_element_type=jnp.float32)

    for which in range(2):
        @pl.when(has_up)
        def _():
            sent(which, zs_sem, {"seq": seq + 2}).wait_send()

        @pl.when(sends_near)
        def _():
            sent(which, ys_sem, {"seq": pair}).wait_send()
    for h in range(heads):
        weight_send(h).wait_send()
    for whose, sem in ((core, es_sem), (other, er_sem)):
        view = early.at[:, half_columns(whose, 0, half)]
        pltpu.make_async_copy(view, view, sem).wait()
    pltpu.make_async_copy(
        att_all.at[:, :, att_columns(0, span)], att_all.at[:, :, att_columns(0, span)], as_sem).wait()
    attended_send(heads - 1).wait_recv()


def finish_kernel(w_last, att_all, early, mine, out_hbm, out_s, sem):
    last = att_all.shape[0] - 1
    span = att_all.shape[2] // 2
    theirs = pl.ds(pl.multiple_of((1 - lax.axis_index("head")) * span, span), span)
    copies = []
    for n, (at, count) in enumerate(column_chunks(mine.shape[1])):
        here = slice(at, at + count)
        out_s[:, here] = (early[:, here].astype(jnp.float32) + (mine[:, here] + jnp.dot(
            att_all[last, :, theirs], w_last[theirs, here],
            preferred_element_type=jnp.float32))).astype(jnp.bfloat16)
        copy = pltpu.make_async_copy(
            out_s.at[:, pl.ds(at, count)], out_hbm.at[:, pl.ds(at, count)], sem.at[n])
        copy.start()
        copies.append(copy)
    for copy in copies:
        copy.wait()


def shards(queries, keys, values, segments, out_weight):
    rows = queries.shape[0]
    assert 2 * rows == ATTENTION_SPAN
    heads = keys.shape[1] // HEAD_SIZE
    query_heads = queries.shape[1] // HEAD_SIZE
    span = query_heads // heads * HEAD_SIZE
    width = out_weight.shape[1]
    seg = segments.reshape(segments.shape[0] // rows, 1, rows)
    dma = pltpu.SemaphoreType.DMA
    anywhere = pl.BlockSpec(memory_space=pltpu.HBM)
    here = pl.BlockSpec(memory_space=pltpu.VMEM)
    bf16, f32 = jnp.bfloat16, jnp.float32
    pieces = heads * 2 * PIECES
    w_last, att_all, early, mine = pl.pallas_call(
        attend_kernel,
        out_shape=(
            pltpu.VMEM((2 * span, width), bf16),
            pltpu.VMEM((heads, rows, 2 * span), bf16),
            pltpu.VMEM((rows, width), bf16),
            pltpu.VMEM((rows, width), f32),
        ),
        in_specs=[anywhere] * 5,
        out_specs=(here,) * 4,
        scratch_shapes=[
            pltpu.VMEM((heads - 1, 2 * span, width // 2), bf16),
            pltpu.VMEM((rows, width // 2), f32),
            pltpu.VMEM(seg.shape, seg.dtype),
            pltpu.VMEM(queries.shape, bf16),
            pltpu.VMEM((3 * rows, keys.shape[1]), bf16),
            pltpu.VMEM((3 * rows, keys.shape[1]), bf16),
            pltpu.VMEM((query_heads, rows, 2 * HEAD_SIZE), f32),
            pltpu.VMEM((query_heads, rows, HEAD_SIZE), f32),
            pltpu.VMEM((query_heads // heads, rows, 2 * rows), bf16),
            pltpu.VMEM((rows, 3 * rows), f32),
            dma((4,)), dma((2,)), dma((pieces,)), dma((2,)), dma((2 * heads,)),
            dma((heads,)), dma((heads,)), dma((heads,)), dma, dma((heads,)), dma, dma,
        ],
        compiler_params=pltpu.CompilerParams(
            collective_id=0, has_side_effects=True, vmem_limit_bytes=34 * 1024 * 1024),
    )(queries, keys, values, pltpu.with_memory_space_constraint(seg, pltpu.HBM), out_weight)
    return pl.pallas_call(
        finish_kernel,
        out_shape=jax.ShapeDtypeStruct((rows, width), bf16),
        in_specs=[here] * 4,
        out_specs=anywhere,
        scratch_shapes=[
            pltpu.VMEM((rows, width), bf16), dma((len(column_chunks(width)),)),
        ],
        compiler_params=pltpu.CompilerParams(vmem_limit_bytes=12 * 1024 * 1024),
    )(w_last, att_all, early, mine)


def solution(mesh):
    placed = (
        P(("groups", "seq"), "head"),
        P(("groups", "seq"), "head"),
        P(("groups", "seq"), "head"),
        P("groups"),
        P("head", None),
    )
    return jax.shard_map(
        shards, mesh=mesh, in_specs=placed, out_specs=P(("groups", "seq"), None), check_vma=False
    )
```
